32 devices in a mesh: grp: 2 (over x), tile: 16 (over z, y, core).
Axes of the slice: x: 2, y: 2, z: 4, core: 2. Of those that a mesh axis runs over, the one named last changes fastest.
Arguments:
- visibility: bfloat16 [32, 16, 2, 256, 256], P('tile', 'grp'), parts along dimension 1, may hold values from -12 to 12
- station_beam: bfloat16 [16, 2, 512, 2048], P('grp', None, 'tile'), parts along dimension 0, may hold values from -4.1875 to 4.1875
- antenna_uvw: float32 [16, 3, 2048], P('grp'), parts along dimension 0, may hold values from -40 to 40
- source_dirs: float32 [2, 4096], P(None, 'tile'), may hold values from -0.4 to 0.4
- source_flux: bfloat16 [8192], P(('grp', 'tile')), parts along dimension 0, may hold values from 0.0029907227 to 0.029907227
- visible_list: int32 [8, 512], P(None, 'tile'), may hold values from 0 to 255
- antenna_flags: int32 [16, 2048], P('grp'), parts along dimension 0, may hold values 0 or 1
Outputs:
- residual: bfloat16 [32, 16, 2, 256, 256], P('tile', 'grp'), parts along dimension 1
- flux_grad: float32 [16, 512], P('grp', 'tile'), parts along dimension 0
The draws below stay inside these ranges and needn't reach their ends.
There are 2 independent parts, one for each index of `grp`. The reference program is written for one: setup_inputs(seed, part) draws one part's arguments, and reference() takes and returns one part's arrays. A program takes and returns all parts, laid end to end along the dimension named above; an argument that names none is the same for every part. Nothing has to cross between parts.
Inputs may be any that keep to these rules, and one draw needn't show every extreme that they name: `visible_list`: entry k of a slot names pool source 256 * (k // 32) + value, a source of its own group. `antenna_flags`: 1 marks a flagged antenna.
All inputs are finite; a program needn't handle non-finite values.
Results may differ from the reference program's by a relative error of at most 0.0034.
Values may be sent and summed in bfloat16 or wider, within the bound.
A program may use at most 192 MiB of HBM per device.

```python
import math
import jax
import jax.numpy as jnp
import numpy as np
from jax import lax

ANTENNAS = 2048
VISIBLE = 512
SLOTS = 8
POOL_DEV = 256
BLOCKS = 8
SPAN = 256
UNITS = 32
PER_GROUP = 32
POOL = 4096


def place_ends(values, stream_key, smallest, top_value):
    longest = values.shape.index(max(values.shape))
    spots = []
    for shift in (0, 1):
        where = [jax.random.randint(jax.random.fold_in(stream_key, axis), (), 0, length) for axis, length in enumerate(values.shape)]
        where[longest] = (where[longest] + shift) % values.shape[longest]
        spots.append(tuple(where))
    return values.at[spots[0]].set(smallest).at[spots[1]].set(top_value)


def level_of(rng, shape, cuts, low, high):
    level = 1.0
    for dim, shards_of in cuts:
        draws = jax.random.uniform(jax.random.fold_in(jax.random.fold_in(rng, 6), dim), (shards_of,), jnp.float32, low / len(cuts), high / len(cuts))
        level = level * jnp.repeat(jnp.exp(draws), shape[dim] // shards_of).reshape((-1,) + (1,) * (len(shape) - 1 - dim))
    return level


def centred(stream_key, shape, scale, most, shards=(), held_as=jnp.bfloat16):
    drawn = scale * jax.random.normal(stream_key, shape, jnp.float32)
    if shards:
        drawn = drawn * level_of(stream_key, shape, shards, -0.22, 0.18)
    return jnp.clip(drawn, -most, most).astype(held_as)


def setup_inputs(seed: int = 0, part: int = 0) -> dict:
    arg_keys = jax.random.split(jax.random.key(seed), 8)
    part_keys = jax.random.split(jax.random.fold_in(arg_keys[7], part), 8)
    visibility = centred(part_keys[0], (UNITS, SLOTS, 2, SPAN, SPAN), 2.0, 12.0, ((0, 16),))
    station_beam = centred(part_keys[1], (SLOTS, 2, VISIBLE, ANTENNAS), 0.7, 4.1875, ((2, 16),))
    antenna_uvw = jnp.clip(jax.random.uniform(part_keys[2], (SLOTS, 3, ANTENNAS), jnp.float32, -40.0, 40.0), -40.0, 40.0)
    source_dirs = jnp.clip(jax.random.uniform(arg_keys[3], (2, POOL), jnp.float32, -0.4, 0.4) * level_of(arg_keys[3], (2, POOL), ((1, 16),), -0.4, 0.0), -0.4, 0.4)
    source_flux = jnp.clip(jnp.exp(math.log(0.029907227) - 2.3025851 * jax.random.uniform(part_keys[4], (POOL,), jnp.float32) ** level_of(part_keys[4], (POOL,), ((0, 16),), -0.2, 0.2)), 0.0029907227, 0.029907227).astype(jnp.bfloat16)
    visible_list = place_ends(jax.random.randint(arg_keys[5], (SLOTS, VISIBLE), 0, POOL_DEV), jax.random.fold_in(arg_keys[5], 1), 0, POOL_DEV - 1).astype(jnp.int32)
    antenna_flags = place_ends((jax.random.randint(part_keys[6], (SLOTS, ANTENNAS), 0, 10) < 1).astype(jnp.int32), jax.random.fold_in(part_keys[6], 1), 0, 1)
    return {"visibility": visibility, "station_beam": station_beam, "antenna_uvw": antenna_uvw, "source_dirs": source_dirs, "source_flux": source_flux, "visible_list": visible_list, "antenna_flags": antenna_flags}


two_pi = 2.0 * math.pi

def unit_table(block_count):
    first_list = []
    second_list = []
    diag_list = []
    for row_block in range(block_count):
        for col_block in range(row_block + 1, block_count):
            first_list.append(row_block)
            second_list.append(col_block)
            diag_list.append(0)
    for pair_index in range(block_count // 2):
        first_list.append(2 * pair_index)
        second_list.append(2 * pair_index + 1)
        diag_list.append(1)
    return (np.array(first_list, np.int32), np.array(second_list, np.int32), np.array(diag_list, np.int32))

def make_factors(station_beam, antenna_uvw, coord_east, coord_north):
    depth_term = jnp.sqrt(1.0 - coord_east * coord_east - coord_north * coord_north) - 1.0
    delay_sum = antenna_uvw[:, 0, None, :] * coord_east[:, :, None] + antenna_uvw[:, 1, None, :] * coord_north[:, :, None] + antenna_uvw[:, 2, None, :] * depth_term[:, :, None]
    phases = two_pi * delay_sum
    cosine = jnp.cos(phases)
    sine = jnp.sin(phases)
    beam_f = station_beam.astype(jnp.float32)
    real_part = beam_f[:, 0] * cosine + beam_f[:, 1] * sine
    imag_part = beam_f[:, 1] * cosine - beam_f[:, 0] * sine
    return jnp.stack([real_part, imag_part], 1).astype(jnp.bfloat16)

def predict(rows_f, cols_f, brightness):
    scaled = (rows_f.astype(jnp.float32) * brightness.astype(jnp.float32)[:, None, :, None]).astype(jnp.bfloat16)
    turned = jnp.stack([scaled[:, 1], -scaled[:, 0]], 1)
    stacked = jnp.stack([scaled, turned], 1).astype(jnp.float32)
    return jnp.einsum('tdckr,tckq->tdrq', stacked, cols_f.astype(jnp.float32))

def pull_back(resid, rows_f, cols_f):
    rstack = jnp.stack([jnp.stack([resid[:, 0], -resid[:, 1]], 1), jnp.stack([resid[:, 1], resid[:, 0]], 1)], 1).astype(jnp.float32)
    pulled = jnp.einsum('tdcrq,tckq->tdkr', rstack, cols_f.astype(jnp.float32))
    return lax.optimization_barrier(jnp.sum(rows_f.astype(jnp.float32) * pulled, axis=(1, 3)))

def reference(visibility, station_beam, antenna_uvw, source_dirs, source_flux, visible_list, antenna_flags):
    group_base = jnp.arange(VISIBLE, dtype=jnp.int32) // PER_GROUP * POOL_DEV
    pool_index = (group_base[None, :] + visible_list).astype(jnp.int32)
    coord_east = jnp.take(source_dirs[0], pool_index)
    coord_north = jnp.take(source_dirs[1], pool_index)
    brightness = jnp.take(source_flux, pool_index)
    factors = make_factors(station_beam, antenna_uvw, coord_east, coord_north)
    keep_all = 1.0 - antenna_flags.astype(jnp.float32)
    first_tab, second_tab, diag_tab = unit_table(BLOCKS)
    first_arr = jnp.asarray(first_tab)
    second_arr = jnp.asarray(second_tab)
    diag_arr = jnp.asarray(diag_tab)
    local_ids = jnp.arange(SPAN, dtype=jnp.int32)
    upper_part = local_ids[:, None] < local_ids[None, :]
    lower_part = local_ids[:, None] > local_ids[None, :]

    def one_unit(unit_id):
        start_one = (first_arr[unit_id] * SPAN).astype(jnp.int32)
        start_two = (second_arr[unit_id] * SPAN).astype(jnp.int32)
        diag_tile = diag_arr[unit_id] == 1
        block_one = lax.dynamic_slice_in_dim(factors, start_one, SPAN, 3)
        block_two = lax.dynamic_slice_in_dim(factors, start_two, SPAN, 3)
        cols_one = jnp.where(diag_tile, block_one, block_two)
        first_pred = predict(block_one, cols_one, brightness)
        second_pred = predict(block_two, block_two, brightness)
        first_mask = jnp.logical_or(jnp.logical_not(diag_tile), upper_part)
        predicted = jnp.where(first_mask[None, None], first_pred, jnp.swapaxes(second_pred, 2, 3))
        keep_one = lax.dynamic_slice_in_dim(keep_all, start_one, SPAN, 1)
        keep_two = lax.dynamic_slice_in_dim(keep_all, start_two, SPAN, 1)
        upper_f = upper_part.astype(jnp.float32)
        lower_f = lower_part.astype(jnp.float32)
        off_weight = keep_one[:, :, None] * keep_two[:, None, :]
        diag_weight = upper_f[None] * keep_one[:, :, None] * keep_one[:, None, :] + lower_f[None] * keep_two[:, :, None] * keep_two[:, None, :]
        weights = jnp.where(diag_tile, diag_weight, off_weight)
        vis_unit = lax.dynamic_index_in_dim(visibility, unit_id, 0, keepdims=False)
        residual = (weights[:, None] * (vis_unit.astype(jnp.float32) - predicted)).astype(jnp.bfloat16)
        zero_res = jnp.zeros_like(residual)
        first_res = jnp.where(first_mask[None, None], residual, zero_res)
        second_sel = jnp.logical_and(diag_tile, lower_part)
        second_res = jnp.swapaxes(jnp.where(second_sel[None, None], residual, zero_res), 2, 3)
        partial_value = pull_back(first_res, block_one, cols_one) + pull_back(second_res, block_two, block_two)
        return (residual, partial_value)
    residual, partial_value = lax.map(one_unit, jnp.arange(UNITS, dtype=jnp.int32))
    flux_grad = lax.optimization_barrier(jnp.sum(partial_value, 0)) * (-1.0 / (8.0 * ANTENNAS))
    return (residual, flux_grad)
```

```python
import functools
import math

import jax
import jax.numpy as jnp
from jax import lax
from jax.experimental import pallas as pl
from jax.experimental.pallas import tpu as pltpu
from jax.sharding import PartitionSpec as P

BLOCKS = 8
MESH = pl.DeviceIdType.MESH

two_pi = 2.0 * math.pi


def sin_cos_turns(turns):
    quarter = jnp.floor(turns * 4.0 + 0.5)
    angle = two_pi * (turns - quarter * 0.25)
    a2 = angle * angle
    sn = angle * (1.0 + a2 * (-1.0 / 6 + a2 * (1.0 / 120 + a2 * (-1.0 / 5040 + a2 * (1.0 / 362880)))))
    cs = 1.0 + a2 * (-0.5 + a2 * (1.0 / 24 + a2 * (-1.0 / 720 + a2 * (1.0 / 40320 - a2 * (1.0 / 3628800)))))
    kind = quarter - 4.0 * jnp.floor(quarter * 0.25)
    odd = jnp.logical_or(kind == 1.0, kind == 3.0)
    sine = jnp.where(odd, cs, sn)
    cosine = jnp.where(odd, sn, cs)
    sine = jnp.where(kind >= 2.0, -sine, sine)
    cosine = jnp.where(jnp.logical_or(kind == 1.0, kind == 2.0), -cosine, cosine)
    return sine, cosine


def unit_blocks(unit_id):
    pairs = BLOCKS * (BLOCKS - 1) // 2
    first = jnp.int32(0)
    start = jnp.int32(0)
    offset = 0
    for row in range(1, BLOCKS - 1):
        offset += BLOCKS - row
        first = jnp.where(unit_id >= offset, jnp.int32(row), first)
        start = jnp.where(unit_id >= offset, jnp.int32(offset), start)
    second = unit_id - start + first + 1
    diag = unit_id >= pairs
    first = jnp.where(diag, 2 * (unit_id - pairs), first)
    second = jnp.where(diag, 2 * (unit_id - pairs) + 1, second)
    return first, second, diag


def unit_table():
    pairs = [(p, q) for p in range(BLOCKS) for q in range(p + 1, BLOCKS)]
    return pairs + [(2 * n, 2 * n + 1) for n in range(BLOCKS // 2)]


class Plan:
    def __init__(self, Z, Y, units):
        table = unit_table()
        chips = Z * Y
        self.moves = {}
        self.turn_up = [0] * chips
        self.turn_down = [0] * chips
        if (Z, Y, units) == (4, 2, 2):
            self.moves = dict(MOVES)
            self.turn_up = list(TURN_UP)
            self.turn_down = list(TURN_DOWN)
        T = 2 * chips
        self.worker = [self.moves.get(u, u // units) for u in range(len(table))]
        self.kept = [[self.worker[t * units + u] == t for t in range(T)] for u in range(units)]
        self.extra = [-1] * T
        for u, t in self.moves.items():
            self.extra[t] = u
        need = [set() for _ in range(chips)]
        for u, t in enumerate(self.worker):
            need[t // 2] |= set(table[u])
        rows = [set().union(*need[z * Y:(z + 1) * Y]) for z in range(Z)]
        above = [set().union(*rows[z + 1:]) for z in range(Z)]
        below = [set().union(*rows[:z]) for z in range(Z)]

        def runs(b):
            out = []
            for k in sorted(b):
                if out and out[-1][0] + out[-1][1] == k:
                    out[-1] = (out[-1][0], out[-1][1] + 1)
                else:
                    out.append((k, 1))
            return tuple(out)

        each_chip = range(chips)
        self.up = [runs(above[c // Y]) for c in each_chip]
        self.down = [runs(below[c // Y]) for c in each_chip]
        self.from_below = [self.up[c - Y] if c >= Y else () for c in each_chip]
        self.from_above = [self.down[c + Y] if c + Y < chips else () for c in each_chip]
        self.need = [runs(need[c]) for c in each_chip]
        pair = [c ^ 1 if Y == 2 else c for c in each_chip]
        self.across = [runs(need[pair[c]]) for c in each_chip]

        def turned(c, up, down):
            b = set(need[pair[c]])
            if up:
                b |= above[c // Y]
            if down:
                b |= below[c // Y]
            return runs(b)

        self.first = {}
        for up in (False, True):
            for down in (False, True):
                self.first[up, down] = [turned(c, up, down) for c in each_chip]
        self.pair = pair


MOVES = {28: 10, 29: 8}
TURN_UP = (1,0,4,5,0,8,0,0)
TURN_DOWN = (0,)*8
AHEAD = 1
HOP_LAG = 1
Y_LAG = 1
FINAL_EXTRA = 0


def count(runs):
    return sum(n for _, n in runs)


def kernel(
    dims, plan, beam, uvw, dirs, pool_flux, listed, flags, vis, res, flux,
    own, bacc, bright, gath, ball, work, flx, frecv,
    r_sem, su, sd, sy, sc, lc, vsem, osem, bs, br, fs, fr, ms, mr, ks, kr,
):
    Z, Y, slots, units, per_group, span, scale = dims
    T = Z * Y * 2
    me = lax.axis_index("tile")
    core = me % 2
    chip = me // 2
    y = chip % Y
    z = chip // Y
    yother = (y + 1) % Y

    def dev(zi, yi, ci):
        return (zi * Y + yi) * 2 + ci

    other = dev(z, y, 1 - core)

    def lookup(table, index):
        base = max(set(table), key=table.count)
        out = jnp.int32(base)
        for k, v in enumerate(table):
            if v != base:
                out = jnp.where(index == k, jnp.int32(v), out)
        return out

    def by_chip(table, body, when=None):
        groups = {}
        for k, v in enumerate(table):
            groups.setdefault(v, []).append(k)
        for v, members in groups.items():
            if not v:
                continue
            cond = when
            if len(groups) > 1:
                here = functools.reduce(jnp.logical_or, [chip == k for k in members])
                cond = here if when is None else jnp.logical_and(when, here)
            if cond is None:
                body(v)
            else:
                pl.when(cond)(functools.partial(body, v))

    def both(*conds):
        return functools.reduce(jnp.logical_and, conds)

    def rc(src, dst, target, send, recv):
        return pltpu.make_async_remote_copy(
            src_ref=src, dst_ref=dst, send_sem=send, recv_sem=recv,
            device_id={"tile": target}, device_id_type=MESH,
        )

    def piece(s, sh, b0, n, mine):
        return own.at[s, pl.ds(b0, n)] if mine else gath.at[s, pl.ds(b0, n), sh]

    def send(table, s, sh, target, sem, mine, when=None):
        def go(runs):
            for b0, n in runs:
                rc(piece(s, sh, b0, n, mine), gath.at[s, pl.ds(b0, n), sh], target, sem, r_sem.at[s, sh]).start()
        by_chip(table, go, when)

    def sent(table, s, sem, when=None):
        def go(runs):
            n = count(runs)
            src = own.at[s, pl.ds(0, n)]
            rc(src, gath.at[s, pl.ds(0, n), me], other, sem, r_sem.at[s, me]).wait_send()
        by_chip(table, go, when)

    def arrived(table, s, sh, when=None):
        def go(runs):
            n = count(runs)
            dst = gath.at[s, pl.ds(0, n), sh]
            rc(dst, dst, other, lc.at[s], r_sem.at[s, sh]).wait_recv()
        by_chip(table, go, when)

    def each(body, steps, start=0):
        def step(i, carry):
            body(i)
            return carry
        lax.fori_loop(start, steps, step, 0)

    def turns_up(zi, yi, s):
        return s >= slots - lookup(plan.turn_up, zi * Y + yi)

    def turns_down(zi, yi, s):
        return s >= slots - lookup(plan.turn_down, zi * Y + yi)

    any_up = any(plan.turn_up)
    any_down = any(plan.turn_down)

    def vis_copy(s, u):
        return pltpu.make_async_copy(vis.at[u, s], work.at[s, u], vsem.at[s, u])

    def res_copy(s, u):
        return pltpu.make_async_copy(work.at[s, u], res.at[u, s], osem.at[s, u])

    def kept(u):
        return lookup([int(k) for k in plan.kept[u]], me) == 1

    all_kept = [all(k) for k in plan.kept]
    extra_id = lookup(plan.extra, me)
    extra_home = extra_id // units
    extra_row = extra_id % units

    def lend(s, u):
        target = lookup([plan.worker[t * units + u] for t in range(T)], me)
        return rc(vis.at[u, s], work.at[s, units], target, ms.at[s, u], mr.at[s])

    def give_back(s):
        return rc(work.at[s, units], res.at[extra_row, s], extra_home, ks.at[s], kr.at[s, extra_row])

    barrier = pltpu.get_barrier_semaphore()
    each(lambda k: pl.semaphore_signal(
        barrier, inc=1, device_id={"tile": (me + k + 1) % T}, device_id_type=MESH), T - 1)

    def up(s, zi, yi, mine=False, when=None):
        cond = z < Z - 1 if when is None else both(z < Z - 1, when)
        send(plan.up, s, dev(zi, yi, core), dev(z + 1, y, core), su.at[s, zi * Y + yi], mine, cond)

    def down(s, zi, yi, mine=False, when=None):
        cond = z > 0 if when is None else both(z > 0, when)
        send(plan.down, s, dev(zi, yi, core), dev(z - 1, y, core), sd.at[s, zi * Y + yi], mine, cond)

    def mate(s, zi, yi, mine=False, when=None):
        send(plan.need, s, dev(zi, yi, core), other, sc.at[s, zi * Y + yi], mine, when)

    def pick_first(zi, yi, s, body):
        for u_ in ((False, True) if any_up else (False,)):
            for d_ in ((False, True) if any_down else (False,)):
                conds = []
                if any_up:
                    t = turns_up(zi, yi, s)
                    conds.append(t if u_ else jnp.logical_not(t))
                if any_down:
                    t = turns_down(zi, yi, s)
                    conds.append(t if d_ else jnp.logical_not(t))
                body(plan.first[u_, d_], both(*conds) if conds else None)

    def own_step(s):
        up(s, z, y, True)
        down(s, z, y, True)
        if Y > 1:
            pick_first(z, y, s, lambda table, cond: send(
                table, s, me, dev(z, yother, core), sy.at[s, z], True, cond))
        mate(s, z, y, True)
        pltpu.make_async_copy(own.at[s], gath.at[s, :, me], lc.at[s]).start()

    pool_size = dirs.shape[1]
    slot_lane = lax.broadcasted_iota(jnp.int32, (per_group, 128), 1)
    pool_lane = lax.broadcasted_iota(jnp.int32, (per_group, pool_size), 1).astype(jnp.float32)

    def make_factors(s):
        at_slot = slot_lane == s
        index = jnp.sum(jnp.where(at_slot, listed[...], 0.0), axis=1, keepdims=True)
        chosen = pool_lane == index

        def pick(row):
            return jnp.sum(jnp.where(chosen, row, 0.0), axis=1, keepdims=True)

        east = pick(dirs[0:1, :])
        north = pick(dirs[1:2, :])
        bacc[...] += jnp.where(at_slot, pick(pool_flux[...]), 0.0)
        depth = jnp.sqrt(1.0 - east * east - north * north) - 1.0
        for b in range(BLOCKS):
            cut = slice(b * span, (b + 1) * span)
            turns = uvw[s, 0:1, cut] * east + uvw[s, 1:2, cut] * north + uvw[s, 2:3, cut] * depth
            sine, cosine = sin_cos_turns(turns)
            b0 = beam[s, 0, :, cut].astype(jnp.float32)
            b1 = beam[s, 1, :, cut].astype(jnp.float32)
            own[s, b, :per_group] = (b0 * cosine + b1 * sine).astype(jnp.bfloat16)
            own[s, b, per_group:] = (b1 * cosine - b0 * sine).astype(jnp.bfloat16)

    bacc[...] = jnp.zeros_like(bacc)
    make_factors(0)
    pl.semaphore_wait(barrier, T - 1)
    ahead = min(AHEAD, slots)

    def lend_step(s):
        for u in range(units):
            if not all_kept[u]:
                pl.when(jnp.logical_not(kept(u)))(lambda: lend(s, u).start())

    def make_and_send(s):
        make_factors(s + 1)

        @pl.when(s < ahead)
        def _():
            own_step(s)
            lend_step(s)
    each(make_and_send, slots - 1)
    bright[...] = bacc[...].astype(jnp.bfloat16)
    flx[...] = jnp.zeros_like(flx)
    if ahead == slots:
        own_step(slots - 1)
        lend_step(slots - 1)

    def bright_step(k):
        target = (me + k + 1) % T
        rc(bright, ball.at[me], target, bs.at[k], br.at[me]).start()
    each(bright_step, T - 1)
    ball[me] = bright[...]

    def vis_step(s):
        for u in range(units):
            if all_kept[u]:
                vis_copy(s, u).start()
            else:
                pl.when(kept(u))(lambda: vis_copy(s, u).start())
    each(vis_step, slots)

    def z_one(zi, s, upward):
        sh = dev(zi, y, core)
        arrived(plan.from_below if upward else plan.from_above, s, sh)
        (up if upward else down)(s, zi, y)
        if Y > 1:
            cond = None
            if upward and any_up:
                cond = jnp.logical_not(turns_up(zi, y, s))
            if not upward and any_down:
                cond = jnp.logical_not(turns_down(zi, y, s))
            send(plan.across, s, sh, dev(z, yother, core), sy.at[s, zi], False, cond)
        mate(s, zi, y)

    def z_step(d, s):
        pl.when(z - d >= 0)(lambda: z_one(z - d, s, True))
        pl.when(z + d < Z)(lambda: z_one(z + d, s, False))

    def y_far(zi, s, upward):
        sh = dev(zi, yother, core)
        if any_up if upward else any_down:
            turned = (turns_up if upward else turns_down)(zi, yother, s)

            @pl.when(turned)
            def _():
                arrived(plan.from_below if upward else plan.from_above, s, sh)
                (up if upward else down)(s, zi, yother)
            arrived(plan.need, s, sh, jnp.logical_not(turned))
        else:
            arrived(plan.need, s, sh)
        mate(s, zi, yother)

    def y_near(s):
        sh = dev(z, yother, core)

        def go(table, cond):
            arrived([table[plan.pair[c]] for c in range(Z * Y)], s, sh, cond)
        pick_first(z, yother, s, go)
        if any_up:
            up(s, z, yother, when=turns_up(z, yother, s))
        if any_down:
            down(s, z, yother, when=turns_down(z, yother, s))
        mate(s, z, yother)

    def y_step(d, s):
        if Y == 1:
            return
        if d == 0:
            y_near(s)
            return
        pl.when(z - d >= 0)(lambda: y_far(z - d, s, True))
        pl.when(z + d < Z)(lambda: y_far(z + d, s, False))

    def bright_wait(k):
        src = (me + k + 1) % T
        rc(bright, ball.at[src], other, bs.at[k], br.at[src]).wait_recv()

    rows = T * 2 * per_group
    split = (T, 2, per_group, span)

    def turn(a):
        a4 = a.reshape(split)
        return jnp.concatenate([a4[:, 1:], -a4[:, :1]], axis=1).reshape(rows, span)

    def tn(a, b):
        return lax.dot_general(a, b, (((0,), (0,)), ((), ())), preferred_element_type=jnp.float32)

    def nt(a, b):
        return lax.dot_general(a, b, (((1,), (1,)), ((), ())), preferred_element_type=jnp.float32)

    def nn(a, b):
        return lax.dot_general(a, b, (((1,), (0,)), ((), ())), preferred_element_type=jnp.float32)

    def compute(s):
        lane = lax.broadcasted_iota(jnp.int32, (T, per_group, 128), 2)
        here = lane == s
        bcol = jnp.sum(jnp.where(here, ball[...].astype(jnp.float32), 0.0), axis=2, keepdims=True)

        def block(b):
            return gath[s, b].reshape(rows, span)

        def scaled_of(f):
            f4 = f.reshape(split).astype(jnp.float32)
            return (f4 * bcol[:, None]).astype(jnp.bfloat16).reshape(rows, span)

        def keep_row(t, b):
            start = pl.multiple_of(b * span, span)
            return 1.0 - flags[pl.ds(t, 1), pl.ds(start, span)].astype(jnp.float32)

        def flag_rows(b):
            return jnp.broadcast_to(keep_row(s, b), (span, span)).T

        def add_flux(x, u, v):
            w = x.astype(jnp.float32) * u + turn(x).astype(jnp.float32) * v
            w = w.reshape(split)
            w = jnp.sum(w, axis=1)
            total = jnp.sum(w, axis=2, keepdims=True)
            flx[...] += jnp.where(here, total, 0.0)

        def unit(u, unit_id):
            p, q, diag = unit_blocks(unit_id)

            @pl.when(jnp.logical_not(diag))
            def _():
                x = block(p)
                c = block(q)
                sx = scaled_of(x)
                w = flag_rows(p) * keep_row(s, q)
                rre = (w * (work[s, u, 0].astype(jnp.float32) - tn(sx, c))).astype(jnp.bfloat16)
                rim = (w * (work[s, u, 1].astype(jnp.float32) - tn(turn(sx), c))).astype(jnp.bfloat16)
                work[s, u, 0] = rre
                work[s, u, 1] = rim
                add_flux(x, nt(c, rre), nt(c, rim))

            @pl.when(diag)
            def _():
                x = block(p)
                c = block(q)
                rid = lax.broadcasted_iota(jnp.int32, (span, span), 0)
                cid = lax.broadcasted_iota(jnp.int32, (span, span), 1)
                hi = rid < cid
                lo = rid > cid
                sx = scaled_of(x)
                sb = scaled_of(c)
                pre = jnp.where(hi, tn(sx, x), tn(c, sb))
                pim = jnp.where(hi, tn(turn(sx), x), tn(c, turn(sb)))
                w = jnp.where(hi, flag_rows(p) * keep_row(s, p), 0.0) + jnp.where(
                    lo, flag_rows(q) * keep_row(s, q), 0.0)
                rre = (w * (work[s, u, 0].astype(jnp.float32) - pre)).astype(jnp.bfloat16)
                rim = (w * (work[s, u, 1].astype(jnp.float32) - pim)).astype(jnp.bfloat16)
                work[s, u, 0] = rre
                work[s, u, 1] = rim
                zero = jnp.zeros((span, span), jnp.float32)

                def part(r, m):
                    return jnp.where(m, r.astype(jnp.float32), zero).astype(jnp.bfloat16)
                add_flux(x, nt(x, part(rre, hi)), nt(x, part(rim, hi)))
                add_flux(c, nn(c, part(rre, lo)), nn(c, part(rim, lo)))

        def run(u):
            lent = u == units
            active = jnp.logical_and(lent, extra_id >= 0)
            for k in range(units):
                mine = u == k
                active = jnp.logical_or(active, mine if all_kept[k] else jnp.logical_and(mine, kept(k)))

            @pl.when(active)
            def _():
                @pl.when(lent)
                def _():
                    rc(work.at[s, units], work.at[s, units], other, ks.at[s], mr.at[s]).wait_recv()

                @pl.when(jnp.logical_not(lent))
                def _():
                    vis_copy(s, jnp.where(lent, 0, u)).wait()
                unit(u, jnp.where(lent, extra_id, me * units + u))

                @pl.when(lent)
                def _():
                    give_back(s).start()

                @pl.when(jnp.logical_not(lent))
                def _():
                    res_copy(s, jnp.where(lent, 0, u)).start()

        if plan.moves:
            each(lambda k: run(units - k), units + 1)
        else:
            each(run, units)

    def last_step(s):
        @pl.when(s == 0)
        def _():
            each(bright_wait, T - 1)
        pltpu.make_async_copy(own.at[s], gath.at[s, :, me], lc.at[s]).wait()

        def mates(i):
            arrived(plan.need, s, 2 * i + 1 - core)
        each(mates, T // 2)
        compute(s)

    hop_lag = HOP_LAG
    final_lag = max(Z - 2, 0) * hop_lag + Y_LAG + FINAL_EXTRA

    def at(t, lag, body):
        s = t - lag

        @pl.when(jnp.logical_and(s >= 0, s < slots))
        def _():
            body(s)

    def tick(t):
        if ahead < slots:
            def more(s):
                own_step(s)
                lend_step(s)
            at(t, -ahead, more)
        at(t, 0, lambda s: y_step(0, s))
        for d in range(1, Z):
            at(t, (d - 1) * hop_lag, functools.partial(z_step, d))
            at(t, (d - 1) * hop_lag + Y_LAG, functools.partial(y_step, d))
        at(t, final_lag, last_step)

    each(tick, slots + final_lag)

    def flux_step(k):
        target = (me + k + 1) % T
        rc(flx.at[target], frecv.at[me], target, fs.at[k], fr.at[me]).start()
    each(flux_step, T - 1)
    frecv[me] = flx[me]

    def tidy(s):
        for u in range(units):
            if all_kept[u]:
                res_copy(s, u).wait()
            else:
                pl.when(kept(u))(lambda: res_copy(s, u).wait())

                @pl.when(jnp.logical_not(kept(u)))
                def _():
                    lend(s, u).wait_send()
                    rc(work.at[s, units], res.at[u, s], other, ks.at[s], kr.at[s, u]).wait_recv()
        if plan.moves:
            @pl.when(extra_id >= 0)
            def _():
                rc(work.at[s, units], res.at[0, s], other, ks.at[s], kr.at[s, 0]).wait_send()

        def from_row(zi):
            def z_sent(yi, extra_up, extra_down):
                sent(plan.up, s, su.at[s, zi * Y + yi], both(zi <= z, z < Z - 1, *extra_up))
                sent(plan.down, s, sd.at[s, zi * Y + yi], both(zi >= z, z > 0, *extra_down))

            z_sent(y, (), ())
            if Y > 1:
                if any_up:
                    sent(plan.up, s, su.at[s, zi * Y + yother], both(zi <= z, z < Z - 1, turns_up(zi, yother, s)))
                if any_down:
                    sent(plan.down, s, sd.at[s, zi * Y + yother], both(zi >= z, z > 0, turns_down(zi, yother, s)))

                @pl.when(zi == z)
                def _():
                    pick_first(z, y, s, lambda table, cond: sent(table, s, sy.at[s, zi], cond))
                below = zi < z
                if any_up:
                    below = both(below, jnp.logical_not(turns_up(zi, y, s)))
                sent(plan.across, s, sy.at[s, zi], below)
                above = zi > z
                if any_down:
                    above = both(above, jnp.logical_not(turns_down(zi, y, s)))
                sent(plan.across, s, sy.at[s, zi], above)
            for yi in range(Y):
                sent(plan.need, s, sc.at[s, zi * Y + yi])
        each(from_row, Z)
    each(tidy, slots)

    def small_wait(k):
        src = (me + k + 1) % T
        rc(bright, ball.at[me], src, bs.at[k], br.at[me]).wait_send()
        one = rc(flx.at[src], frecv.at[src], src, fs.at[k], fr.at[src])
        one.wait_send()
        one.wait_recv()
    each(small_wait, T - 1)
    flux[...] = jnp.sum(frecv[...], axis=0) * scale


def per_device(
    layout, visibility, station_beam, antenna_uvw, source_dirs, source_flux, visible_list, antenna_flags
):
    Z, Y = layout
    T = lax.axis_size("tile")
    units, slots, _, span, _ = visibility.shape
    per_group = station_beam.shape[2]
    antennas = station_beam.shape[3]
    listed = jnp.pad(visible_list.astype(jnp.float32).T, ((0, 0), (0, 128 - slots)))
    pool_flux = source_flux.astype(jnp.float32)[None]
    dims = (Z, Y, slots, units, per_group, span, -1.0 / (8.0 * antennas))
    plan = Plan(Z, Y, units)
    vmem = pl.BlockSpec(memory_space=pltpu.VMEM)
    hbm = pl.BlockSpec(memory_space=pl.ANY)
    dma = pltpu.SemaphoreType.DMA
    residual, flux = pl.pallas_call(
        functools.partial(kernel, dims, plan),
        name="predict_pull",
        out_shape=(
            jax.ShapeDtypeStruct(visibility.shape, jnp.bfloat16),
            jax.ShapeDtypeStruct((per_group, 128), jnp.float32),
        ),
        in_specs=[vmem] * 6 + [hbm],
        out_specs=(hbm, vmem),
        scratch_shapes=[
            pltpu.VMEM((slots, BLOCKS, 2 * per_group, span), jnp.bfloat16),
            pltpu.VMEM((per_group, 128), jnp.float32),
            pltpu.VMEM((per_group, 128), jnp.bfloat16),
            pltpu.VMEM((slots, BLOCKS, T, 2 * per_group, span), jnp.bfloat16),
            pltpu.VMEM((T, per_group, 128), jnp.bfloat16),
            pltpu.VMEM((slots, units + 1, 2, span, span), jnp.bfloat16),
            pltpu.VMEM((T, per_group, 128), jnp.float32),
            pltpu.VMEM((T, per_group, 128), jnp.float32),
            dma((slots, T)),
            dma((slots, Z * Y)),
            dma((slots, Z * Y)),
            dma((slots, Z)),
            dma((slots, Z * Y)),
            dma((slots,)),
            dma((slots, units)),
            dma((slots, units)),
            dma((T,)),
            dma((T,)),
            dma((T,)),
            dma((T,)),
            dma((slots, units)),
            dma((slots,)),
            dma((slots,)),
            dma((slots, units)),
        ],
        compiler_params=pltpu.CompilerParams(
            collective_id=0, has_side_effects=True, vmem_limit_bytes=64 * 1024 * 1024 - 2 * 65536
        ),
    )(station_beam, antenna_uvw, source_dirs, pool_flux, listed, antenna_flags, visibility)
    return residual, flux[:, :slots].T


def layout_of(mesh):
    count = mesh.shape["tile"]
    line = mesh.devices.reshape(-1, count)[0]
    places = [getattr(d, "coords", None) for d in line]
    fast = 1
    if all(c is not None for c in places):
        fast = max(1, len({tuple(c)[1] for c in places}))
    if (count // 2) % fast or fast > 2:
        fast = 1
    return count // 2 // fast, fast


def solution(mesh):
    return jax.shard_map(
        functools.partial(per_device, layout_of(mesh)),
        mesh=mesh,
        in_specs=(
            P("tile", "grp", None, None, None),
            P("grp", None, "tile", None),
            P("grp", None, None),
            P(None, "tile"),
            P(("grp", "tile")),
            P(None, "tile"),
            P("grp", None),
        ),
        out_specs=(P("tile", "grp", None, None, None), P("grp", "tile")),
        check_vma=False,
    )
```

```python
import functools
import math

import jax
import jax.numpy as jnp
from jax import lax
from jax.experimental import pallas as pl
from jax.experimental.pallas import tpu as pltpu
from jax.sharding import PartitionSpec as P

BLOCKS = 8
MESH = pl.DeviceIdType.MESH

two_pi = 2.0 * math.pi


def sin_cos_turns(turns):
    quarter = jnp.floor(turns * 4.0 + 0.5)
    angle = two_pi * (turns - quarter * 0.25)
    a2 = angle * angle
    sn = angle * (1.0 + a2 * (-1.0 / 6 + a2 * (1.0 / 120 + a2 * (-1.0 / 5040 + a2 * (1.0 / 362880)))))
    cs = 1.0 + a2 * (-0.5 + a2 * (1.0 / 24 + a2 * (-1.0 / 720 + a2 * (1.0 / 40320 - a2 * (1.0 / 3628800)))))
    kind = quarter - 4.0 * jnp.floor(quarter * 0.25)
    odd = jnp.logical_or(kind == 1.0, kind == 3.0)
    sine = jnp.where(odd, cs, sn)
    cosine = jnp.where(odd, sn, cs)
    sine = jnp.where(kind >= 2.0, -sine, sine)
    cosine = jnp.where(jnp.logical_or(kind == 1.0, kind == 2.0), -cosine, cosine)
    return sine, cosine


def unit_blocks(unit_id):
    pairs = BLOCKS * (BLOCKS - 1) // 2
    first = jnp.int32(0)
    start = jnp.int32(0)
    offset = 0
    for row in range(1, BLOCKS - 1):
        offset += BLOCKS - row
        first = jnp.where(unit_id >= offset, jnp.int32(row), first)
        start = jnp.where(unit_id >= offset, jnp.int32(offset), start)
    second = unit_id - start + first + 1
    diag = unit_id >= pairs
    first = jnp.where(diag, 2 * (unit_id - pairs), first)
    second = jnp.where(diag, 2 * (unit_id - pairs) + 1, second)
    return first, second, diag


def unit_table():
    pairs = [(p, q) for p in range(BLOCKS) for q in range(p + 1, BLOCKS)]
    return pairs + [(2 * n, 2 * n + 1) for n in range(BLOCKS // 2)]


class Plan:
    def __init__(self, Z, Y, units):
        table = unit_table()
        chips = Z * Y
        self.moves = {}
        self.turn_up = [0] * chips
        self.turn_down = [0] * chips
        if (Z, Y, units) == (4, 2, 2):
            self.moves = dict(MOVES)
            self.turn_up = list(TURN_UP)
            self.turn_down = list(TURN_DOWN)
        T = 2 * chips
        self.worker = [self.moves.get(u, u // units) for u in range(len(table))]
        self.kept = [[self.worker[t * units + u] == t for t in range(T)] for u in range(units)]
        self.extra = [-1] * T
        for u, t in self.moves.items():
            self.extra[t] = u
        need = [set() for _ in range(chips)]
        for u, t in enumerate(self.worker):
            need[t // 2] |= set(table[u])
        rows = [set().union(*need[z * Y:(z + 1) * Y]) for z in range(Z)]
        above = [set().union(*rows[z + 1:]) for z in range(Z)]
        below = [set().union(*rows[:z]) for z in range(Z)]

        def runs(b):
            out = []
            for k in sorted(b):
                if out and out[-1][0] + out[-1][1] == k:
                    out[-1] = (out[-1][0], out[-1][1] + 1)
                else:
                    out.append((k, 1))
            return tuple(out)

        each_chip = range(chips)
        self.up = [runs(above[c // Y]) for c in each_chip]
        self.down = [runs(below[c // Y]) for c in each_chip]
        self.from_below = [self.up[c - Y] if c >= Y else () for c in each_chip]
        self.from_above = [self.down[c + Y] if c + Y < chips else () for c in each_chip]
        self.need = [runs(need[c]) for c in each_chip]
        pair = [c ^ 1 if Y == 2 else c for c in each_chip]
        self.across = [runs(need[pair[c]]) for c in each_chip]

        def turned(c, up, down):
            b = set(need[pair[c]])
            if up:
                b |= above[c // Y]
            if down:
                b |= below[c // Y]
            return runs(b)

        self.first = {}
        for up in (False, True):
            for down in (False, True):
                self.first[up, down] = [turned(c, up, down) for c in each_chip]
        self.pair = pair


MOVES = {28: 10, 29: 8}
TURN_UP = (1, 0, 4, 5, 0, 8, 0, 0)
TURN_DOWN = (0, 0, 0, 0, 0, 0, 0, 0)
AHEAD = 2
HOP_LAG = 1
Y_LAG = 2
NEAR_LAG = 0
FINAL_EXTRA = 0


def count(runs):
    return sum(n for _, n in runs)


def kernel(
    dims, plan, beam, uvw, dirs, pool_flux, listed, flags, vis, res, flux,
    own, bacc, bright, gath, ball, work, flx, frecv,
    r_sem, su, sd, sy, sc, lc, vsem, osem, bs, br, fs, fr, ms, mr, ks, kr,
):
    Z, Y, slots, units, per_group, span, scale = dims
    T = Z * Y * 2
    me = lax.axis_index("tile")
    core = me % 2
    chip = me // 2
    y = chip % Y
    z = chip // Y
    yother = (y + 1) % Y

    def dev(zi, yi, ci):
        return (zi * Y + yi) * 2 + ci

    other = dev(z, y, 1 - core)

    def lookup(table, index):
        base = max(set(table), key=table.count)
        out = jnp.int32(base)
        for k, v in enumerate(table):
            if v != base:
                out = jnp.where(index == k, jnp.int32(v), out)
        return out

    def by_chip(table, body, when=None):
        groups = {}
        for k, v in enumerate(table):
            groups.setdefault(v, []).append(k)
        for v, members in groups.items():
            if not v:
                continue
            cond = when
            if len(groups) > 1:
                here = functools.reduce(jnp.logical_or, [chip == k for k in members])
                cond = here if when is None else jnp.logical_and(when, here)
            if cond is None:
                body(v)
            else:
                pl.when(cond)(functools.partial(body, v))

    def both(*conds):
        return functools.reduce(jnp.logical_and, conds)

    def rc(src, dst, target, send, recv):
        return pltpu.make_async_remote_copy(
            src_ref=src, dst_ref=dst, send_sem=send, recv_sem=recv,
            device_id={"tile": target}, device_id_type=MESH,
        )

    def piece(s, sh, b0, n, mine):
        return own.at[s, pl.ds(b0, n)] if mine else gath.at[s, pl.ds(b0, n), sh]

    def send(table, s, sh, target, sem, mine, when=None):
        def go(runs):
            for b0, n in runs:
                rc(piece(s, sh, b0, n, mine), gath.at[s, pl.ds(b0, n), sh], target, sem, r_sem.at[s, sh]).start()
        by_chip(table, go, when)

    def sent(table, s, sem, when=None):
        def go(runs):
            n = count(runs)
            src = own.at[s, pl.ds(0, n)]
            rc(src, gath.at[s, pl.ds(0, n), me], other, sem, r_sem.at[s, me]).wait_send()
        by_chip(table, go, when)

    def arrived(table, s, sh, when=None):
        def go(runs):
            n = count(runs)
            dst = gath.at[s, pl.ds(0, n), sh]
            rc(dst, dst, other, lc.at[s], r_sem.at[s, sh]).wait_recv()
        by_chip(table, go, when)

    def each(body, steps, start=0):
        def step(i, carry):
            body(i)
            return carry
        lax.fori_loop(start, steps, step, 0)

    def turns_up(zi, yi, s):
        return s >= slots - lookup(plan.turn_up, zi * Y + yi)

    def turns_down(zi, yi, s):
        return s >= slots - lookup(plan.turn_down, zi * Y + yi)

    any_up = any(plan.turn_up)
    any_down = any(plan.turn_down)

    def vis_copy(s, u):
        return pltpu.make_async_copy(vis.at[u, s], work.at[s, u], vsem.at[s, u])

    def res_copy(s, u):
        return pltpu.make_async_copy(work.at[s, u], res.at[u, s], osem.at[s, u])

    def kept(u):
        return lookup([int(k) for k in plan.kept[u]], me) == 1

    all_kept = [all(k) for k in plan.kept]
    extra_id = lookup(plan.extra, me)
    extra_home = extra_id // units
    extra_row = extra_id % units

    def lend(s, u):
        target = lookup([plan.worker[t * units + u] for t in range(T)], me)
        return rc(vis.at[u, s], work.at[s, units], target, ms.at[s, u], mr.at[s])

    def give_back(s):
        return rc(work.at[s, units], res.at[extra_row, s], extra_home, ks.at[s], kr.at[s, extra_row])

    barrier = pltpu.get_barrier_semaphore()
    each(lambda k: pl.semaphore_signal(
        barrier, inc=1, device_id={"tile": (me + k + 1) % T}, device_id_type=MESH), T - 1)

    def up(s, zi, yi, mine=False, when=None):
        cond = z < Z - 1 if when is None else both(z < Z - 1, when)
        send(plan.up, s, dev(zi, yi, core), dev(z + 1, y, core), su.at[s, zi * Y + yi], mine, cond)

    def down(s, zi, yi, mine=False, when=None):
        cond = z > 0 if when is None else both(z > 0, when)
        send(plan.down, s, dev(zi, yi, core), dev(z - 1, y, core), sd.at[s, zi * Y + yi], mine, cond)

    def mate(s, zi, yi, mine=False, when=None):
        send(plan.need, s, dev(zi, yi, core), other, sc.at[s, zi * Y + yi], mine, when)

    def pick_first(zi, yi, s, body):
        for u_ in ((False, True) if any_up else (False,)):
            for d_ in ((False, True) if any_down else (False,)):
                conds = []
                if any_up:
                    t = turns_up(zi, yi, s)
                    conds.append(t if u_ else jnp.logical_not(t))
                if any_down:
                    t = turns_down(zi, yi, s)
                    conds.append(t if d_ else jnp.logical_not(t))
                body(plan.first[u_, d_], both(*conds) if conds else None)

    def own_step(s):
        up(s, z, y, True)
        down(s, z, y, True)
        if Y > 1:
            pick_first(z, y, s, lambda table, cond: send(
                table, s, me, dev(z, yother, core), sy.at[s, z], True, cond))
        mate(s, z, y, True)
        pltpu.make_async_copy(own.at[s], gath.at[s, :, me], lc.at[s]).start()

    pool_size = dirs.shape[1]
    slot_lane = lax.broadcasted_iota(jnp.int32, (per_group, 128), 1)
    pool_lane = lax.broadcasted_iota(jnp.int32, (per_group, pool_size), 1).astype(jnp.float32)

    same = lax.broadcasted_iota(jnp.int32, (per_group, per_group), 0) == lax.broadcasted_iota(
        jnp.int32, (per_group, per_group), 1)

    def make_factors(s):
        at_slot = slot_lane == s
        row = listed[pl.ds(s, 1), :].astype(jnp.float32)
        index = jnp.sum(jnp.where(same, row, 0.0), axis=1, keepdims=True)
        chosen = pool_lane == index

        def pick(row):
            return jnp.sum(jnp.where(chosen, row, 0.0), axis=1, keepdims=True)

        east = pick(dirs[0:1, :])
        north = pick(dirs[1:2, :])
        bacc[...] += jnp.where(at_slot, pick(pool_flux[...].astype(jnp.float32)), 0.0)
        depth = jnp.sqrt(1.0 - east * east - north * north) - 1.0
        for b in range(BLOCKS):
            cut = slice(b * span, (b + 1) * span)
            turns = uvw[0, pl.ds(s, 1), cut] * east + uvw[1, pl.ds(s, 1), cut] * north + uvw[2, pl.ds(s, 1), cut] * depth
            sine, cosine = sin_cos_turns(turns)
            b0 = beam[s, 0, :, cut].astype(jnp.float32)
            b1 = beam[s, 1, :, cut].astype(jnp.float32)
            own[s, b, :per_group] = (b0 * cosine + b1 * sine).astype(jnp.bfloat16)
            own[s, b, per_group:] = (b1 * cosine - b0 * sine).astype(jnp.bfloat16)

    bacc[...] = jnp.zeros_like(bacc)
    make_factors(0)
    pl.semaphore_wait(barrier, T - 1)
    ahead = min(AHEAD, slots)

    def lend_step(s):
        for u in range(units):
            if not all_kept[u]:
                pl.when(jnp.logical_not(kept(u)))(lambda: lend(s, u).start())

    def make_and_send(s):
        make_factors(s + 1)

        @pl.when(s < ahead)
        def _():
            own_step(s)
            lend_step(s)
    each(make_and_send, slots - 1)
    bright[...] = bacc[...].astype(jnp.bfloat16)
    flx[...] = jnp.zeros_like(flx)
    if ahead == slots:
        own_step(slots - 1)
        lend_step(slots - 1)

    def bright_step(k):
        target = (me + k + 1) % T
        rc(bright, ball.at[me], target, bs.at[k], br.at[me]).start()
    each(bright_step, T - 1)
    ball[me] = bright[...]

    def vis_step(s):
        for u in range(units):
            if all_kept[u]:
                vis_copy(s, u).start()
            else:
                pl.when(kept(u))(lambda: vis_copy(s, u).start())
    each(vis_step, slots)

    def z_one(zi, s, upward):
        sh = dev(zi, y, core)
        arrived(plan.from_below if upward else plan.from_above, s, sh)
        (up if upward else down)(s, zi, y)
        if Y > 1:
            cond = None
            if upward and any_up:
                cond = jnp.logical_not(turns_up(zi, y, s))
            if not upward and any_down:
                cond = jnp.logical_not(turns_down(zi, y, s))
            send(plan.across, s, sh, dev(z, yother, core), sy.at[s, zi], False, cond)
        mate(s, zi, y)

    def z_step(d, s):
        pl.when(z - d >= 0)(lambda: z_one(z - d, s, True))
        pl.when(z + d < Z)(lambda: z_one(z + d, s, False))

    def y_far(zi, s, upward):
        sh = dev(zi, yother, core)
        if any_up if upward else any_down:
            turned = (turns_up if upward else turns_down)(zi, yother, s)

            @pl.when(turned)
            def _():
                arrived(plan.from_below if upward else plan.from_above, s, sh)
                (up if upward else down)(s, zi, yother)
            arrived(plan.need, s, sh, jnp.logical_not(turned))
        else:
            arrived(plan.need, s, sh)
        mate(s, zi, yother)

    def y_near(s):
        sh = dev(z, yother, core)

        def go(table, cond):
            arrived([table[plan.pair[c]] for c in range(Z * Y)], s, sh, cond)
        pick_first(z, yother, s, go)
        if any_up:
            up(s, z, yother, when=turns_up(z, yother, s))
        if any_down:
            down(s, z, yother, when=turns_down(z, yother, s))
        mate(s, z, yother)

    def y_step(d, s):
        if Y == 1:
            return
        if d == 0:
            y_near(s)
            return
        pl.when(z - d >= 0)(lambda: y_far(z - d, s, True))
        pl.when(z + d < Z)(lambda: y_far(z + d, s, False))

    def bright_wait(k):
        src = (me + k + 1) % T
        rc(bright, ball.at[src], other, bs.at[k], br.at[src]).wait_recv()

    rows = T * 2 * per_group
    split = (T, 2, per_group, span)

    def turn(a):
        a4 = a.reshape(split)
        return jnp.concatenate([a4[:, 1:], -a4[:, :1]], axis=1).reshape(rows, span)

    def tn(a, b):
        return lax.dot_general(a, b, (((0,), (0,)), ((), ())), preferred_element_type=jnp.float32)

    def nt(a, b):
        return lax.dot_general(a, b, (((1,), (1,)), ((), ())), preferred_element_type=jnp.float32)

    def nn(a, b):
        return lax.dot_general(a, b, (((1,), (0,)), ((), ())), preferred_element_type=jnp.float32)

    def compute(s):
        lane = lax.broadcasted_iota(jnp.int32, (T, per_group, 128), 2)
        here = lane == s
        bcol = jnp.sum(jnp.where(here, ball[...].astype(jnp.float32), 0.0), axis=2, keepdims=True)

        def block(b):
            return gath[s, b].reshape(rows, span)

        def scaled_of(f):
            f4 = f.reshape(split).astype(jnp.float32)
            return (f4 * bcol[:, None]).astype(jnp.bfloat16).reshape(rows, span)

        def keep_row(t, b):
            start = pl.multiple_of(b * span, span)
            return 1.0 - flags[pl.ds(t, 1), pl.ds(start, span)].astype(jnp.float32)

        def flag_rows(b):
            return jnp.broadcast_to(keep_row(s, b), (span, span)).T

        def add_flux(x, u, v):
            w = x.astype(jnp.float32) * u + turn(x).astype(jnp.float32) * v
            w = w.reshape(split)
            w = jnp.sum(w, axis=1)
            total = jnp.sum(w, axis=2, keepdims=True)
            flx[...] += jnp.where(here, total, 0.0)

        def unit(u, unit_id):
            p, q, diag = unit_blocks(unit_id)

            @pl.when(jnp.logical_not(diag))
            def _():
                x = block(p)
                c = block(q)
                sx = scaled_of(x)
                w = flag_rows(p) * keep_row(s, q)
                rre = (w * (work[s, u, 0].astype(jnp.float32) - tn(sx, c))).astype(jnp.bfloat16)
                rim = (w * (work[s, u, 1].astype(jnp.float32) - tn(turn(sx), c))).astype(jnp.bfloat16)
                work[s, u, 0] = rre
                work[s, u, 1] = rim
                add_flux(x, nt(c, rre), nt(c, rim))

            @pl.when(diag)
            def _():
                x = block(p)
                c = block(q)
                rid = lax.broadcasted_iota(jnp.int32, (span, span), 0)
                cid = lax.broadcasted_iota(jnp.int32, (span, span), 1)
                hi = rid < cid
                lo = rid > cid
                sx = scaled_of(x)
                sb = scaled_of(c)
                pre = jnp.where(hi, tn(sx, x), tn(c, sb))
                pim = jnp.where(hi, tn(turn(sx), x), tn(c, turn(sb)))
                w = jnp.where(hi, flag_rows(p) * keep_row(s, p), 0.0) + jnp.where(
                    lo, flag_rows(q) * keep_row(s, q), 0.0)
                rre = (w * (work[s, u, 0].astype(jnp.float32) - pre)).astype(jnp.bfloat16)
                rim = (w * (work[s, u, 1].astype(jnp.float32) - pim)).astype(jnp.bfloat16)
                work[s, u, 0] = rre
                work[s, u, 1] = rim
                zero = jnp.zeros((span, span), jnp.float32)

                def part(r, m):
                    return jnp.where(m, r.astype(jnp.float32), zero).astype(jnp.bfloat16)
                add_flux(x, nt(x, part(rre, hi)), nt(x, part(rim, hi)))
                add_flux(c, nn(c, part(rre, lo)), nn(c, part(rim, lo)))

        def run(u):
            lent = u == units
            active = jnp.logical_and(lent, extra_id >= 0)
            for k in range(units):
                mine = u == k
                active = jnp.logical_or(active, mine if all_kept[k] else jnp.logical_and(mine, kept(k)))

            @pl.when(active)
            def _():
                @pl.when(lent)
                def _():
                    rc(work.at[s, units], work.at[s, units], other, ks.at[s], mr.at[s]).wait_recv()

                @pl.when(jnp.logical_not(lent))
                def _():
                    vis_copy(s, jnp.where(lent, 0, u)).wait()
                unit(u, jnp.where(lent, extra_id, me * units + u))

                @pl.when(lent)
                def _():
                    give_back(s).start()

                @pl.when(jnp.logical_not(lent))
                def _():
                    res_copy(s, jnp.where(lent, 0, u)).start()

        if plan.moves:
            each(lambda k: run(units - k), units + 1)
        else:
            each(run, units)

    def last_step(s):
        @pl.when(s == 0)
        def _():
            each(bright_wait, T - 1)
        pltpu.make_async_copy(own.at[s], gath.at[s, :, me], lc.at[s]).wait()

        def mates(i):
            arrived(plan.need, s, 2 * i + 1 - core)
        each(mates, T // 2)
        compute(s)

    hop_lag = HOP_LAG
    final_lag = max(Z - 2, 0) * hop_lag + Y_LAG + FINAL_EXTRA

    def at(t, lag, body):
        s = t - lag

        @pl.when(jnp.logical_and(s >= 0, s < slots))
        def _():
            body(s)

    def tick(t):
        if ahead < slots:
            def more(s):
                own_step(s)
                lend_step(s)
            at(t, -ahead, more)
        for d in range(1, Z):
            at(t, (d - 1) * hop_lag, functools.partial(z_step, d))
        at(t, NEAR_LAG, lambda s: y_step(0, s))
        for d in range(1, Z):
            at(t, (d - 1) * hop_lag + Y_LAG, functools.partial(y_step, d))
        at(t, final_lag, last_step)

    each(tick, slots + final_lag)

    def flux_step(k):
        target = (me + k + 1) % T
        rc(flx.at[target], frecv.at[me], target, fs.at[k], fr.at[me]).start()
    each(flux_step, T - 1)
    frecv[me] = flx[me]

    def tidy(s):
        for u in range(units):
            if all_kept[u]:
                res_copy(s, u).wait()
            else:
                pl.when(kept(u))(lambda: res_copy(s, u).wait())

                @pl.when(jnp.logical_not(kept(u)))
                def _():
                    lend(s, u).wait_send()
                    rc(work.at[s, units], res.at[u, s], other, ks.at[s], kr.at[s, u]).wait_recv()
        if plan.moves:
            @pl.when(extra_id >= 0)
            def _():
                rc(work.at[s, units], res.at[0, s], other, ks.at[s], kr.at[s, 0]).wait_send()

        def from_row(zi):
            def z_sent(yi, extra_up, extra_down):
                sent(plan.up, s, su.at[s, zi * Y + yi], both(zi <= z, z < Z - 1, *extra_up))
                sent(plan.down, s, sd.at[s, zi * Y + yi], both(zi >= z, z > 0, *extra_down))

            z_sent(y, (), ())
            if Y > 1:
                if any_up:
                    sent(plan.up, s, su.at[s, zi * Y + yother], both(zi <= z, z < Z - 1, turns_up(zi, yother, s)))
                if any_down:
                    sent(plan.down, s, sd.at[s, zi * Y + yother], both(zi >= z, z > 0, turns_down(zi, yother, s)))

                @pl.when(zi == z)
                def _():
                    pick_first(z, y, s, lambda table, cond: sent(table, s, sy.at[s, zi], cond))
                below = zi < z
                if any_up:
                    below = both(below, jnp.logical_not(turns_up(zi, y, s)))
                sent(plan.across, s, sy.at[s, zi], below)
                above = zi > z
                if any_down:
                    above = both(above, jnp.logical_not(turns_down(zi, y, s)))
                sent(plan.across, s, sy.at[s, zi], above)
            for yi in range(Y):
                sent(plan.need, s, sc.at[s, zi * Y + yi])
        each(from_row, Z)
    each(tidy, slots)

    def small_wait(k):
        src = (me + k + 1) % T
        rc(bright, ball.at[me], src, bs.at[k], br.at[me]).wait_send()
        one = rc(flx.at[src], frecv.at[src], src, fs.at[k], fr.at[src])
        one.wait_send()
        one.wait_recv()
    each(small_wait, T - 1)
    flux[...] = (jnp.sum(frecv[...], axis=0) * scale).T[:slots]


def per_device(
    layout, visibility, station_beam, antenna_uvw, source_dirs, source_flux, visible_list, antenna_flags
):
    Z, Y = layout
    T = lax.axis_size("tile")
    units, slots, _, span, _ = visibility.shape
    per_group = station_beam.shape[2]
    antennas = station_beam.shape[3]
    dims = (Z, Y, slots, units, per_group, span, -1.0 / (8.0 * antennas))
    plan = Plan(Z, Y, units)
    vmem = pl.BlockSpec(memory_space=pltpu.VMEM)
    hbm = pl.BlockSpec(memory_space=pl.ANY)
    dma = pltpu.SemaphoreType.DMA
    residual, flux = pl.pallas_call(
        functools.partial(kernel, dims, plan),
        name="predict_pull",
        out_shape=(
            pltpu.VMEM(visibility.shape, jnp.bfloat16),
            pltpu.VMEM((slots, per_group), jnp.float32),
        ),
        in_specs=[vmem] * 6 + [hbm],
        out_specs=(vmem, vmem),
        scratch_shapes=[
            pltpu.VMEM((slots, BLOCKS, 2 * per_group, span), jnp.bfloat16),
            pltpu.VMEM((per_group, 128), jnp.float32),
            pltpu.VMEM((per_group, 128), jnp.bfloat16),
            pltpu.VMEM((slots, BLOCKS, T, 2 * per_group, span), jnp.bfloat16),
            pltpu.VMEM((T, per_group, 128), jnp.bfloat16),
            pltpu.VMEM((slots, units + 1, 2, span, span), jnp.bfloat16),
            pltpu.VMEM((T, per_group, 128), jnp.float32),
            pltpu.VMEM((T, per_group, 128), jnp.float32),
            dma((slots, T)),
            dma((slots, Z * Y)),
            dma((slots, Z * Y)),
            dma((slots, Z)),
            dma((slots, Z * Y)),
            dma((slots,)),
            dma((slots, units)),
            dma((slots, units)),
            dma((T,)),
            dma((T,)),
            dma((T,)),
            dma((T,)),
            dma((slots, units)),
            dma((slots,)),
            dma((slots,)),
            dma((slots, units)),
        ],
        compiler_params=pltpu.CompilerParams(
            collective_id=0, has_side_effects=True, vmem_limit_bytes=54 * 1024 * 1024
        ),
    )(station_beam, antenna_uvw.transpose(1, 0, 2), source_dirs, source_flux[None], visible_list, antenna_flags, visibility)
    return residual, flux


def layout_of(mesh):
    count = mesh.shape["tile"]
    line = mesh.devices.reshape(-1, count)[0]
    places = [getattr(d, "coords", None) for d in line]
    fast = 1
    if all(c is not None for c in places):
        fast = max(1, len({tuple(c)[1] for c in places}))
    if (count // 2) % fast or fast > 2:
        fast = 1
    return count // 2 // fast, fast


def solution(mesh):
    return jax.shard_map(
        functools.partial(per_device, layout_of(mesh)),
        mesh=mesh,
        in_specs=(
            P("tile", "grp", None, None, None),
            P("grp", None, "tile", None),
            P("grp", None, None),
            P(None, "tile"),
            P(("grp", "tile")),
            P(None, "tile"),
            P("grp", None),
        ),
        out_specs=(P("tile", "grp", None, None, None), P("grp", "tile")),
        check_vma=False,
    )
```

```python
import functools
import math

import jax
import jax.numpy as jnp
from jax import lax
from jax.experimental import pallas as pl
from jax.experimental.pallas import tpu as pltpu
from jax.sharding import PartitionSpec as P

BLOCKS = 8
MESH = pl.DeviceIdType.MESH

two_pi = 2.0 * math.pi


def sin_cos_turns(turns):
    quarter = jnp.floor(turns * 4.0 + 0.5)
    angle = two_pi * (turns - quarter * 0.25)
    a2 = angle * angle
    sn = angle * (1.0 + a2 * (-1.0 / 6 + a2 * (1.0 / 120 + a2 * (-1.0 / 5040 + a2 * (1.0 / 362880)))))
    cs = 1.0 + a2 * (-0.5 + a2 * (1.0 / 24 + a2 * (-1.0 / 720 + a2 * (1.0 / 40320 - a2 * (1.0 / 3628800)))))
    kind = quarter - 4.0 * jnp.floor(quarter * 0.25)
    odd = jnp.logical_or(kind == 1.0, kind == 3.0)
    sine = jnp.where(odd, cs, sn)
    cosine = jnp.where(odd, sn, cs)
    sine = jnp.where(kind >= 2.0, -sine, sine)
    cosine = jnp.where(jnp.logical_or(kind == 1.0, kind == 2.0), -cosine, cosine)
    return sine, cosine


def unit_blocks(unit_id):
    pairs = BLOCKS * (BLOCKS - 1) // 2
    first = jnp.int32(0)
    start = jnp.int32(0)
    offset = 0
    for row in range(1, BLOCKS - 1):
        offset += BLOCKS - row
        first = jnp.where(unit_id >= offset, jnp.int32(row), first)
        start = jnp.where(unit_id >= offset, jnp.int32(offset), start)
    second = unit_id - start + first + 1
    diag = unit_id >= pairs
    first = jnp.where(diag, 2 * (unit_id - pairs), first)
    second = jnp.where(diag, 2 * (unit_id - pairs) + 1, second)
    return first, second, diag


def unit_table():
    pairs = [(p, q) for p in range(BLOCKS) for q in range(p + 1, BLOCKS)]
    return pairs + [(2 * n, 2 * n + 1) for n in range(BLOCKS // 2)]


class Plan:
    def __init__(self, Z, Y, units):
        table = unit_table()
        chips = Z * Y
        self.moves = {}
        self.turn_up = [0] * chips
        self.turn_down = [0] * chips
        if (Z, Y, units) == (4, 2, 2):
            self.moves = dict(MOVES)
            self.turn_up = list(TURN_UP)
            self.turn_down = list(TURN_DOWN)
        T = 2 * chips
        self.worker = [self.moves.get(u, u // units) for u in range(len(table))]
        self.kept = [[self.worker[t * units + u] == t for t in range(T)] for u in range(units)]
        self.extra = [-1] * T
        for u, t in self.moves.items():
            self.extra[t] = u
        need = [set() for _ in range(chips)]
        for u, t in enumerate(self.worker):
            need[t // 2] |= set(table[u])
        rows = [set().union(*need[z * Y:(z + 1) * Y]) for z in range(Z)]
        above = [set().union(*rows[z + 1:]) for z in range(Z)]
        below = [set().union(*rows[:z]) for z in range(Z)]

        def runs(b):
            out = []
            for k in sorted(b):
                if out and out[-1][0] + out[-1][1] == k:
                    out[-1] = (out[-1][0], out[-1][1] + 1)
                else:
                    out.append((k, 1))
            return tuple(out)

        each_chip = range(chips)
        self.up = [runs(above[c // Y]) for c in each_chip]
        self.down = [runs(below[c // Y]) for c in each_chip]
        self.from_below = [self.up[c - Y] if c >= Y else () for c in each_chip]
        self.from_above = [self.down[c + Y] if c + Y < chips else () for c in each_chip]
        self.need = [runs(need[c]) for c in each_chip]
        pair = [c ^ 1 if Y == 2 else c for c in each_chip]
        self.across = [runs(need[pair[c]]) for c in each_chip]

        def turned(c, up, down):
            b = set(need[pair[c]])
            if up:
                b |= above[c // Y]
            if down:
                b |= below[c // Y]
            return runs(b)

        self.first = {}
        for up in (False, True):
            for down in (False, True):
                self.first[up, down] = [turned(c, up, down) for c in each_chip]
        self.pair = pair


MOVES = {28: 10, 29: 8, 3: 4, 6: 7}
TURN_UP = (6, 2, 0, 4, 0, 0, 0, 0)
TURN_DOWN = (0, 0, 0, 0, 0, 0, 0, 1)
END_AHEAD = 2
AHEAD = 2
SIDE_AHEAD = 2
LEND_AHEAD = 2
HOP_LAG = 1
Y_LAG = 2
NEAR_LAG = 0
FINAL_EXTRA = 0


def count(runs):
    return sum(n for _, n in runs)


def kernel(
    dims, plan, beam, uvw, dirs, pool_flux, listed, flags, vis, res, flux,
    own, bacc, bright, gath, ball, work, flx, fsend, frecv,
    r_sem, su, sd, sy, sc, lc, vsem, osem, bs, br, fs, fr, ms, mr, ks, kr,
):
    Z, Y, slots, units, per_group, span, scale = dims
    T = Z * Y * 2
    me = lax.axis_index("tile")
    core = me % 2
    chip = me // 2
    y = chip % Y
    z = chip // Y
    yother = (y + 1) % Y

    def dev(zi, yi, ci):
        return (zi * Y + yi) * 2 + ci

    other = dev(z, y, 1 - core)

    def when(cond):
        def run_if(body):
            if cond is None or cond is True:
                body()
            elif cond is not False:
                pl.when(cond)(body)
        return run_if

    def negate(cond):
        return (not cond) if isinstance(cond, bool) else jnp.logical_not(cond)

    def lookup(table, index):
        if isinstance(index, int):
            return table[index]
        base = max(set(table), key=table.count)
        out = jnp.int32(base)
        for k, v in enumerate(table):
            if v != base:
                out = jnp.where(index == k, jnp.int32(v), out)
        return out

    def by_chip(table, body, cond=None):
        if isinstance(chip, int):
            if table[chip]:
                when(cond)(functools.partial(body, table[chip]))
            return
        groups = {}
        for k, v in enumerate(table):
            groups.setdefault(v, []).append(k)
        for v, members in groups.items():
            if not v:
                continue
            here = True
            if len(groups) > 1:
                here = functools.reduce(jnp.logical_or, [chip == k for k in members])
            when(both(here, cond))(functools.partial(body, v))

    def both(*conds):
        kept_conds = [c for c in conds if c is not None and c is not True]
        if any(c is False for c in kept_conds):
            return False
        return functools.reduce(jnp.logical_and, kept_conds) if kept_conds else True

    def placed(k, body):
        nonlocal chip, z, y, yother, other
        saved = chip, z, y, yother, other
        chip, z, y = k, k // Y, k % Y
        yother = (y + 1) % Y
        other = dev(z, y, 1 - core)
        body()
        chip, z, y, yother, other = saved

    def rc(src, dst, target, send, recv):
        return pltpu.make_async_remote_copy(
            src_ref=src, dst_ref=dst, send_sem=send, recv_sem=recv,
            device_id={"tile": target}, device_id_type=MESH,
        )

    def piece(s, sh, b0, n, mine):
        return own.at[s, pl.ds(b0, n)] if mine else gath.at[s, sh, pl.ds(b0, n)]

    def send(table, s, sh, target, sem, mine, cond=None):
        def go(runs):
            for b0, n in runs:
                rc(piece(s, sh, b0, n, mine), gath.at[s, sh, pl.ds(b0, n)], target, sem, r_sem.at[s, sh]).start()
        by_chip(table, go, cond)

    def sent(table, s, sem, cond=None):
        def go(runs):
            n = count(runs)
            src = own.at[s, pl.ds(0, n)]
            rc(src, gath.at[s, me, pl.ds(0, n)], other, sem, r_sem.at[s, me]).wait_send()
        by_chip(table, go, cond)

    def arrived(table, s, sh, cond=None):
        def go(runs):
            n = count(runs)
            dst = gath.at[s, sh, pl.ds(0, n)]
            rc(dst, dst, other, lc.at[s], r_sem.at[s, sh]).wait_recv()
        by_chip(table, go, cond)

    def each(body, steps, start=0):
        def step(i, carry):
            body(i)
            return carry
        lax.fori_loop(start, steps, step, 0)

    def spread(s, n):
        if isinstance(n, int) and n in (0, slots):
            return n == slots
        return ((s + 1) * n) // slots > (s * n) // slots

    def turns_up(zi, yi, s):
        return spread(s, lookup(plan.turn_up, zi * Y + yi))

    def turns_down(zi, yi, s):
        return spread(s, lookup(plan.turn_down, zi * Y + yi))

    any_up = any(plan.turn_up)
    any_down = any(plan.turn_down)

    def vis_copy(s, u):
        return pltpu.make_async_copy(vis.at[u, s], work.at[s, u], vsem.at[s, u])

    def res_copy(s, u):
        return pltpu.make_async_copy(work.at[s, u], res.at[u, s], osem.at[s, u])

    def kept(u):
        return lookup([int(k) for k in plan.kept[u]], me) == 1

    all_kept = [all(k) for k in plan.kept]
    extra_id = lookup(plan.extra, me)
    extra_home = extra_id // units
    extra_row = extra_id % units

    def lend(s, u):
        target = lookup([plan.worker[t * units + u] for t in range(T)], me)
        return rc(vis.at[u, s], work.at[s, units], target, ms.at[s, u], mr.at[s])

    def give_back(s):
        return rc(work.at[s, units], res.at[extra_row, s], extra_home, ks.at[s], kr.at[s, extra_row])

    barrier = pltpu.get_barrier_semaphore()
    each(lambda k: pl.semaphore_signal(
        barrier, inc=1, device_id={"tile": (me + k + 1) % T}, device_id_type=MESH), T - 1)

    def up(s, zi, yi, mine=False, cond=None):
        cond = both(z < Z - 1, cond)
        send(plan.up, s, dev(zi, yi, core), dev(z + 1, y, core), su.at[s, zi * Y + yi], mine, cond)

    def down(s, zi, yi, mine=False, cond=None):
        cond = both(z > 0, cond)
        send(plan.down, s, dev(zi, yi, core), dev(z - 1, y, core), sd.at[s, zi * Y + yi], mine, cond)

    def mate(s, zi, yi, mine=False, cond=None):
        send(plan.need, s, dev(zi, yi, core), other, sc.at[s, zi * Y + yi], mine, cond)

    def pick_first(zi, yi, s, body):
        for u_ in ((False, True) if any_up else (False,)):
            for d_ in ((False, True) if any_down else (False,)):
                conds = []
                if any_up:
                    t = turns_up(zi, yi, s)
                    conds.append(t if u_ else negate(t))
                if any_down:
                    t = turns_down(zi, yi, s)
                    conds.append(t if d_ else negate(t))
                body(plan.first[u_, d_], both(*conds) if conds else None)

    def own_z(s):
        up(s, z, y, True)
        down(s, z, y, True)

    def own_side(s):
        if Y > 1:
            pick_first(z, y, s, lambda table, cond: send(
                table, s, me, dev(z, yother, core), sy.at[s, z], True, cond))
        mate(s, z, y, True)
        pltpu.make_async_copy(own.at[s], gath.at[s, me], lc.at[s]).start()

    pool_size = dirs.shape[1]
    slot_lane = lax.broadcasted_iota(jnp.int32, (per_group, 128), 1)
    pool_lane = lax.broadcasted_iota(jnp.int32, (per_group, pool_size), 1).astype(jnp.float32)

    same = lax.broadcasted_iota(jnp.int32, (per_group, per_group), 0) == lax.broadcasted_iota(
        jnp.int32, (per_group, per_group), 1)

    def make_factors(s):
        at_slot = slot_lane == s
        row = listed[pl.ds(s, 1), :].astype(jnp.float32)
        index = jnp.sum(jnp.where(same, row, 0.0), axis=1, keepdims=True)
        chosen = pool_lane == index

        def pick(row):
            return jnp.sum(jnp.where(chosen, row, 0.0), axis=1, keepdims=True)

        east = pick(dirs[0:1, :])
        north = pick(dirs[1:2, :])
        bacc[...] += jnp.where(at_slot, pick(pool_flux[...].astype(jnp.float32)), 0.0)
        depth = jnp.sqrt(1.0 - east * east - north * north) - 1.0
        for b in range(BLOCKS):
            cut = slice(b * span, (b + 1) * span)
            turns = uvw[0, pl.ds(s, 1), cut] * east + uvw[1, pl.ds(s, 1), cut] * north + uvw[2, pl.ds(s, 1), cut] * depth
            sine, cosine = sin_cos_turns(turns)
            b0 = beam[s, 0, :, cut].astype(jnp.float32)
            b1 = beam[s, 1, :, cut].astype(jnp.float32)
            own[s, b, :per_group] = (b0 * cosine + b1 * sine).astype(jnp.bfloat16)
            own[s, b, per_group:] = (b1 * cosine - b0 * sine).astype(jnp.bfloat16)

    bacc[...] = jnp.zeros_like(bacc)
    make_factors(0)
    pl.semaphore_wait(barrier, T - 1)
    def lend_step(s):
        for u in range(units):
            if not all_kept[u]:
                pl.when(jnp.logical_not(kept(u)))(lambda: lend(s, u).start())

    def at_end():
        if isinstance(z, int):
            return z in (0, Z - 1)
        return jnp.logical_or(z == 0, z == Z - 1)

    starts = (
        (min(END_AHEAD, slots), at_end, own_z),
        (min(AHEAD, slots), lambda: negate(at_end()), own_z),
        (min(SIDE_AHEAD, slots), None, own_side),
        (min(LEND_AHEAD, slots), None, lend_step),
    )

    def make_and_send(s):
        make_factors(s + 1)

        for lead, cond, body in starts:
            early = s < lead
            when(both(early, cond and cond()))(functools.partial(body, s))
    each(make_and_send, slots - 1)
    bright[...] = bacc[...].astype(jnp.bfloat16)
    flx[...] = jnp.zeros_like(flx)
    for lead, cond, body in starts:
        if lead == slots:
            when(cond and cond())(functools.partial(body, slots - 1))

    def bright_step(k):
        target = (me + k + 1) % T
        rc(bright, ball.at[me], target, bs.at[k], br.at[me]).start()
    each(bright_step, T - 1)
    ball[me] = bright[...]

    def vis_step(s):
        for u in range(units):
            if all_kept[u]:
                vis_copy(s, u).start()
            else:
                pl.when(kept(u))(lambda: vis_copy(s, u).start())
    each(vis_step, slots)

    def z_one(zi, s, upward):
        sh = dev(zi, y, core)
        arrived(plan.from_below if upward else plan.from_above, s, sh)
        (up if upward else down)(s, zi, y)
        if Y > 1:
            cond = None
            if upward and any_up:
                cond = negate(turns_up(zi, y, s))
            if not upward and any_down:
                cond = negate(turns_down(zi, y, s))
            send(plan.across, s, sh, dev(z, yother, core), sy.at[s, zi], False, cond)
        mate(s, zi, y)

    def z_step(d, s):
        when(z - d >= 0)(lambda: z_one(z - d, s, True))
        when(z + d < Z)(lambda: z_one(z + d, s, False))

    def y_far(zi, s, upward):
        sh = dev(zi, yother, core)
        if any_up if upward else any_down:
            turned = (turns_up if upward else turns_down)(zi, yother, s)

            @when(turned)
            def _():
                arrived(plan.from_below if upward else plan.from_above, s, sh)
                (up if upward else down)(s, zi, yother)
            arrived(plan.need, s, sh, negate(turned))
        else:
            arrived(plan.need, s, sh)
        mate(s, zi, yother)

    def y_near(s):
        sh = dev(z, yother, core)

        def go(table, cond):
            arrived([table[plan.pair[c]] for c in range(Z * Y)], s, sh, cond)
        pick_first(z, yother, s, go)
        if any_up:
            up(s, z, yother, cond=turns_up(z, yother, s))
        if any_down:
            down(s, z, yother, cond=turns_down(z, yother, s))
        mate(s, z, yother)

    def y_step(d, s):
        if Y == 1:
            return
        if d == 0:
            y_near(s)
            return
        when(z - d >= 0)(lambda: y_far(z - d, s, True))
        when(z + d < Z)(lambda: y_far(z + d, s, False))

    def bright_wait(k):
        src = (me + k + 1) % T
        rc(bright, ball.at[src], other, bs.at[k], br.at[src]).wait_recv()

    rows = T * 2 * per_group
    split = (T, 2, per_group, span)

    def turn(a):
        a4 = a.reshape(split)
        return jnp.concatenate([a4[:, 1:], -a4[:, :1]], axis=1).reshape(rows, span)

    def tn(a, b):
        return lax.dot_general(a, b, (((0,), (0,)), ((), ())), preferred_element_type=jnp.float32)

    def nt(a, b):
        return lax.dot_general(a, b, (((1,), (1,)), ((), ())), preferred_element_type=jnp.float32)

    def nn(a, b):
        return lax.dot_general(a, b, (((1,), (0,)), ((), ())), preferred_element_type=jnp.float32)

    def compute(s):
        lane = lax.broadcasted_iota(jnp.int32, (T, per_group, 128), 2)
        here = lane == s
        bcol = jnp.sum(jnp.where(here, ball[...].astype(jnp.float32), 0.0), axis=2, keepdims=True)

        def block(b):
            return gath[s, :, b].reshape(rows, span)

        def scaled_of(f):
            f4 = f.reshape(split).astype(jnp.float32)
            return (f4 * bcol[:, None]).astype(jnp.bfloat16).reshape(rows, span)

        def keep_row(t, b):
            start = pl.multiple_of(b * span, span)
            return 1.0 - flags[pl.ds(t, 1), pl.ds(start, span)].astype(jnp.float32)

        def flag_rows(b):
            return jnp.broadcast_to(keep_row(s, b), (span, span)).T

        def add_flux(x, u, v):
            w = x.astype(jnp.float32) * u + turn(x).astype(jnp.float32) * v
            w = w.reshape(split)
            w = jnp.sum(w, axis=1)
            total = jnp.sum(w, axis=2, keepdims=True)
            flx[...] += jnp.where(here, total, 0.0)

        def unit(u, unit_id):
            p, q, diag = unit_blocks(unit_id)

            @pl.when(jnp.logical_not(diag))
            def _():
                x = block(p)
                c = block(q)
                sx = scaled_of(x)
                w = flag_rows(p) * keep_row(s, q)
                rre = (w * (work[s, u, 0].astype(jnp.float32) - tn(sx, c))).astype(jnp.bfloat16)
                rim = (w * (work[s, u, 1].astype(jnp.float32) - tn(turn(sx), c))).astype(jnp.bfloat16)
                work[s, u, 0] = rre
                work[s, u, 1] = rim
                add_flux(x, nt(c, rre), nt(c, rim))

            @pl.when(diag)
            def _():
                x = block(p)
                c = block(q)
                rid = lax.broadcasted_iota(jnp.int32, (span, span), 0)
                cid = lax.broadcasted_iota(jnp.int32, (span, span), 1)
                hi = rid < cid
                lo = rid > cid
                sx = scaled_of(x)
                sb = scaled_of(c)
                pre = jnp.where(hi, tn(sx, x), tn(c, sb))
                pim = jnp.where(hi, tn(turn(sx), x), tn(c, turn(sb)))
                w = jnp.where(hi, flag_rows(p) * keep_row(s, p), 0.0) + jnp.where(
                    lo, flag_rows(q) * keep_row(s, q), 0.0)
                rre = (w * (work[s, u, 0].astype(jnp.float32) - pre)).astype(jnp.bfloat16)
                rim = (w * (work[s, u, 1].astype(jnp.float32) - pim)).astype(jnp.bfloat16)
                work[s, u, 0] = rre
                work[s, u, 1] = rim
                zero = jnp.zeros((span, span), jnp.float32)

                def part(r, m):
                    return jnp.where(m, r.astype(jnp.float32), zero).astype(jnp.bfloat16)
                add_flux(x, nt(x, part(rre, hi)), nt(x, part(rim, hi)))
                add_flux(c, nn(c, part(rre, lo)), nn(c, part(rim, lo)))

        def run(u):
            lent = u == units
            active = jnp.logical_and(lent, extra_id >= 0)
            for k in range(units):
                mine = u == k
                active = jnp.logical_or(active, mine if all_kept[k] else jnp.logical_and(mine, kept(k)))

            @pl.when(active)
            def _():
                @pl.when(lent)
                def _():
                    rc(work.at[s, units], work.at[s, units], other, ks.at[s], mr.at[s]).wait_recv()

                @pl.when(jnp.logical_not(lent))
                def _():
                    vis_copy(s, jnp.where(lent, 0, u)).wait()
                unit(u, jnp.where(lent, extra_id, me * units + u))

                @pl.when(lent)
                def _():
                    give_back(s).start()

                @pl.when(jnp.logical_not(lent))
                def _():
                    res_copy(s, jnp.where(lent, 0, u)).start()

        if plan.moves:
            each(lambda k: run(units - k), units + 1)
        else:
            each(run, units)

    def last_step(s):
        @pl.when(s == 0)
        def _():
            each(bright_wait, T - 1)
        pltpu.make_async_copy(own.at[s], gath.at[s, me], lc.at[s]).wait()

        compute(s)

    def mates(s):
        if isinstance(chip, int):
            for i in range(T // 2):
                arrived(plan.need, s, 2 * i + 1 - core)
            return
        each(lambda i: arrived(plan.need, s, 2 * i + 1 - core), T // 2)

    hop_lag = HOP_LAG
    final_lag = max(Z - 2, 0) * hop_lag + Y_LAG + FINAL_EXTRA

    def at(t, lag, body, cond=None):
        s = t - lag
        due = jnp.logical_and(s >= 0, s < slots)

        @when(both(due, cond))
        def _():
            body(s)

    def transfers(t):
        for lead, cond, body in starts:
            if lead < slots:
                at(t, -lead, body, cond and cond())
        for d in range(1, Z):
            at(t, (d - 1) * hop_lag, functools.partial(z_step, d))
        at(t, NEAR_LAG, lambda s: y_step(0, s))
        for d in range(1, Z):
            at(t, (d - 1) * hop_lag + Y_LAG, functools.partial(y_step, d))
        at(t, final_lag, mates)

    def tick(t):
        if Z * Y <= 8:
            for k in range(Z * Y):
                pl.when(chip == k)(lambda: placed(k, lambda: transfers(t)))
        else:
            transfers(t)
        at(t, final_lag, last_step)

    each(tick, slots + final_lag)

    sharing = 128 // per_group
    turned_flux = flx[...].reshape(T * per_group, 128).T[:slots]
    for k in range(T // sharing):
        fsend[k] = turned_flux[:, k * 128:(k + 1) * 128]

    def flux_step(k):
        target = (me + k + 1) % T
        rc(fsend.at[target // sharing], frecv.at[me], target, fs.at[k], fr.at[me]).start()
    each(flux_step, T - 1)
    frecv[me] = fsend[me // sharing]

    def tidy(s):
        for u in range(units):
            if all_kept[u]:
                res_copy(s, u).wait()
            else:
                pl.when(kept(u))(lambda: res_copy(s, u).wait())

                @pl.when(jnp.logical_not(kept(u)))
                def _():
                    lend(s, u).wait_send()
                    rc(work.at[s, units], res.at[u, s], other, ks.at[s], kr.at[s, u]).wait_recv()
        if plan.moves:
            @pl.when(extra_id >= 0)
            def _():
                rc(work.at[s, units], res.at[0, s], other, ks.at[s], kr.at[s, 0]).wait_send()

        def from_row(zi):
            def z_sent(yi, extra_up, extra_down):
                sent(plan.up, s, su.at[s, zi * Y + yi], both(zi <= z, z < Z - 1, *extra_up))
                sent(plan.down, s, sd.at[s, zi * Y + yi], both(zi >= z, z > 0, *extra_down))

            z_sent(y, (), ())
            if Y > 1:
                if any_up:
                    sent(plan.up, s, su.at[s, zi * Y + yother], both(zi <= z, z < Z - 1, turns_up(zi, yother, s)))
                if any_down:
                    sent(plan.down, s, sd.at[s, zi * Y + yother], both(zi >= z, z > 0, turns_down(zi, yother, s)))

                @pl.when(zi == z)
                def _():
                    pick_first(z, y, s, lambda table, cond: sent(table, s, sy.at[s, zi], cond))
                below = zi < z
                if any_up:
                    below = both(below, jnp.logical_not(turns_up(zi, y, s)))
                sent(plan.across, s, sy.at[s, zi], below)
                above = zi > z
                if any_down:
                    above = both(above, jnp.logical_not(turns_down(zi, y, s)))
                sent(plan.across, s, sy.at[s, zi], above)
            for yi in range(Y):
                sent(plan.need, s, sc.at[s, zi * Y + yi])
        each(from_row, Z)
    each(tidy, slots)

    def small_wait(k):
        src = (me + k + 1) % T
        rc(bright, ball.at[me], src, bs.at[k], br.at[me]).wait_send()
        one = rc(fsend.at[src // sharing], frecv.at[src], src, fs.at[k], fr.at[src])
        one.wait_send()
        one.wait_recv()
    each(small_wait, T - 1)
    total = jnp.sum(frecv[...], axis=0) * scale
    mine = total[:, :per_group]
    for k in range(1, sharing):
        mine = jnp.where(me % sharing == k, total[:, k * per_group:(k + 1) * per_group], mine)
    flux[...] = mine


def per_device(
    layout, visibility, station_beam, antenna_uvw, source_dirs, source_flux, visible_list, antenna_flags
):
    Z, Y = layout
    T = lax.axis_size("tile")
    units, slots, _, span, _ = visibility.shape
    per_group = station_beam.shape[2]
    antennas = station_beam.shape[3]
    dims = (Z, Y, slots, units, per_group, span, -1.0 / (8.0 * antennas))
    plan = Plan(Z, Y, units)
    vmem = pl.BlockSpec(memory_space=pltpu.VMEM)
    hbm = pl.BlockSpec(memory_space=pl.ANY)
    dma = pltpu.SemaphoreType.DMA
    residual, flux = pl.pallas_call(
        functools.partial(kernel, dims, plan),
        name="predict_pull",
        out_shape=(
            pltpu.VMEM(visibility.shape, jnp.bfloat16),
            pltpu.VMEM((slots, per_group), jnp.float32),
        ),
        in_specs=[vmem] * 6 + [hbm],
        out_specs=(vmem, vmem),
        scratch_shapes=[
            pltpu.VMEM((slots, BLOCKS, 2 * per_group, span), jnp.bfloat16),
            pltpu.VMEM((per_group, 128), jnp.float32),
            pltpu.VMEM((per_group, 128), jnp.bfloat16),
            pltpu.VMEM((slots, T, BLOCKS, 2 * per_group, span), jnp.bfloat16),
            pltpu.VMEM((T, per_group, 128), jnp.bfloat16),
            pltpu.VMEM((slots, units + 1, 2, span, span), jnp.bfloat16),
            pltpu.VMEM((T, per_group, 128), jnp.float32),
            pltpu.VMEM((T * per_group // 128, slots, 128), jnp.float32),
            pltpu.VMEM((T, slots, 128), jnp.float32),
            dma((slots, T)),
            dma((slots, Z * Y)),
            dma((slots, Z * Y)),
            dma((slots, Z)),
            dma((slots, Z * Y)),
            dma((slots,)),
            dma((slots, units)),
            dma((slots, units)),
            dma((T,)),
            dma((T,)),
            dma((T,)),
            dma((T,)),
            dma((slots, units)),
            dma((slots,)),
            dma((slots,)),
            dma((slots, units)),
        ],
        compiler_params=pltpu.CompilerParams(
            collective_id=0, has_side_effects=True, vmem_limit_bytes=54 * 1024 * 1024
        ),
    )(station_beam, antenna_uvw.transpose(1, 0, 2), source_dirs, source_flux[None], visible_list, antenna_flags, visibility)
    return residual, flux


def layout_of(mesh):
    count = mesh.shape["tile"]
    line = mesh.devices.reshape(-1, count)[0]
    places = [getattr(d, "coords", None) for d in line]
    fast = 1
    if all(c is not None for c in places):
        fast = max(1, len({tuple(c)[1] for c in places}))
    if (count // 2) % fast or fast > 2:
        fast = 1
    return count // 2 // fast, fast


def solution(mesh):
    return jax.shard_map(
        functools.partial(per_device, layout_of(mesh)),
        mesh=mesh,
        in_specs=(
            P("tile", "grp", None, None, None),
            P("grp", None, "tile", None),
            P("grp", None, None),
            P(None, "tile"),
            P(("grp", "tile")),
            P(None, "tile"),
            P("grp", None),
        ),
        out_specs=(P("tile", "grp", None, None, None), P("grp", "tile")),
        check_vma=False,
    )
```

```python
import functools
import math

import jax
import jax.numpy as jnp
from jax import lax
from jax.experimental import pallas as pl
from jax.experimental.pallas import tpu as pltpu
from jax.sharding import PartitionSpec as P

BLOCKS = 8
MESH = pl.DeviceIdType.MESH

two_pi = 2.0 * math.pi


def sin_cos_turns(turns):
    quarter = jnp.floor(turns * 4.0 + 0.5)
    angle = two_pi * (turns - quarter * 0.25)
    a2 = angle * angle
    sn = angle * (1.0 + a2 * (-1.0 / 6 + a2 * (1.0 / 120 + a2 * (-1.0 / 5040 + a2 * (1.0 / 362880)))))
    cs = 1.0 + a2 * (-0.5 + a2 * (1.0 / 24 + a2 * (-1.0 / 720 + a2 * (1.0 / 40320 - a2 * (1.0 / 3628800)))))
    kind = quarter - 4.0 * jnp.floor(quarter * 0.25)
    odd = jnp.logical_or(kind == 1.0, kind == 3.0)
    sine = jnp.where(odd, cs, sn)
    cosine = jnp.where(odd, sn, cs)
    sine = jnp.where(kind >= 2.0, -sine, sine)
    cosine = jnp.where(jnp.logical_or(kind == 1.0, kind == 2.0), -cosine, cosine)
    return sine, cosine


def unit_blocks(unit_id):
    pairs = BLOCKS * (BLOCKS - 1) // 2
    first = jnp.int32(0)
    start = jnp.int32(0)
    offset = 0
    for row in range(1, BLOCKS - 1):
        offset += BLOCKS - row
        first = jnp.where(unit_id >= offset, jnp.int32(row), first)
        start = jnp.where(unit_id >= offset, jnp.int32(offset), start)
    second = unit_id - start + first + 1
    diag = unit_id >= pairs
    first = jnp.where(diag, 2 * (unit_id - pairs), first)
    second = jnp.where(diag, 2 * (unit_id - pairs) + 1, second)
    return first, second, diag


def unit_table():
    pairs = [(p, q) for p in range(BLOCKS) for q in range(p + 1, BLOCKS)]
    return pairs + [(2 * n, 2 * n + 1) for n in range(BLOCKS // 2)]


class Plan:
    def __init__(self, Z, Y, units):
        table = unit_table()
        chips = Z * Y
        self.moves = {}
        self.turn_up = [0] * chips
        self.turn_down = [0] * chips
        if (Z, Y, units) == (4, 2, 2):
            self.moves = dict(MOVES)
            self.turn_up = list(TURN_UP)
            self.turn_down = list(TURN_DOWN)
        T = 2 * chips
        self.worker = [self.moves.get(u, u // units) for u in range(len(table))]
        self.kept = [[self.worker[t * units + u] == t for t in range(T)] for u in range(units)]
        self.extra = [-1] * T
        for u, t in self.moves.items():
            self.extra[t] = u
        need = [set() for _ in range(chips)]
        for u, t in enumerate(self.worker):
            need[t // 2] |= set(table[u])
        rows = [set().union(*need[z * Y:(z + 1) * Y]) for z in range(Z)]
        above = [set().union(*rows[z + 1:]) for z in range(Z)]
        below = [set().union(*rows[:z]) for z in range(Z)]

        def runs(b):
            out = []
            for k in sorted(b):
                if out and out[-1][0] + out[-1][1] == k:
                    out[-1] = (out[-1][0], out[-1][1] + 1)
                else:
                    out.append((k, 1))
            return tuple(out)

        each_chip = range(chips)
        self.up = [runs(above[c // Y]) for c in each_chip]
        self.down = [runs(below[c // Y]) for c in each_chip]
        self.from_below = [self.up[c - Y] if c >= Y else () for c in each_chip]
        self.from_above = [self.down[c + Y] if c + Y < chips else () for c in each_chip]
        self.need = [runs(need[c]) for c in each_chip]
        pair = [c ^ 1 if Y == 2 else c for c in each_chip]
        self.across = [runs(need[pair[c]]) for c in each_chip]

        def turned(c, up, down):
            b = set(need[pair[c]])
            if up:
                b |= above[c // Y]
            if down:
                b |= below[c // Y]
            return runs(b)

        self.first = {}
        for up in (False, True):
            for down in (False, True):
                self.first[up, down] = [turned(c, up, down) for c in each_chip]
        self.pair = pair


MOVES = {28: 10, 29: 8, 3: 4, 6: 7}
TURN_UP = (6, 2, 0, 4, 0, 0, 0, 0)
TURN_DOWN = (0, 0, 0, 0, 0, 0, 0, 1)
END_AHEAD = 2
AHEAD = 2
SIDE_AHEAD = 2
LEND_AHEAD = 2
HOP_LAG = 1
Y_LAG = 2
NEAR_LAG = 0
FINAL_EXTRA = 0


def count(runs):
    return sum(n for _, n in runs)


def kernel(
    dims, plan, beam, uvw, dirs, pool_flux, listed, flags, vis, res, flux,
    own, bacc, bright, gath, ball, work, flx, fsend, frecv, bcols,
    r_sem, su, sd, sy, sc, lc, vsem, osem, bs, br, fs, fr, ms, mr, ks, kr,
):
    Z, Y, slots, units, per_group, span, scale = dims
    T = Z * Y * 2
    me = lax.axis_index("tile")
    core = me % 2
    chip = me // 2
    y = chip % Y
    z = chip // Y
    yother = (y + 1) % Y

    def dev(zi, yi, ci):
        return (zi * Y + yi) * 2 + ci

    other = dev(z, y, 1 - core)

    def when(cond):
        def run_if(body):
            if cond is None or cond is True:
                body()
            elif cond is not False:
                pl.when(cond)(body)
        return run_if

    def negate(cond):
        return (not cond) if isinstance(cond, bool) else jnp.logical_not(cond)

    def lookup(table, index):
        if isinstance(index, int):
            return table[index]
        base = max(set(table), key=table.count)
        out = jnp.int32(base)
        for k, v in enumerate(table):
            if v != base:
                out = jnp.where(index == k, jnp.int32(v), out)
        return out

    def by_chip(table, body, cond=None):
        if isinstance(chip, int):
            if table[chip]:
                when(cond)(functools.partial(body, table[chip]))
            return
        groups = {}
        for k, v in enumerate(table):
            groups.setdefault(v, []).append(k)
        for v, members in groups.items():
            if not v:
                continue
            here = True
            if len(groups) > 1:
                here = functools.reduce(jnp.logical_or, [chip == k for k in members])
            when(both(here, cond))(functools.partial(body, v))

    def both(*conds):
        kept_conds = [c for c in conds if c is not None and c is not True]
        if any(c is False for c in kept_conds):
            return False
        return functools.reduce(jnp.logical_and, kept_conds) if kept_conds else True

    def placed(k, body):
        nonlocal chip, z, y, yother, other
        saved = chip, z, y, yother, other
        chip, z, y = k, k // Y, k % Y
        yother = (y + 1) % Y
        other = dev(z, y, 1 - core)
        body()
        chip, z, y, yother, other = saved

    def rc(src, dst, target, send, recv):
        return pltpu.make_async_remote_copy(
            src_ref=src, dst_ref=dst, send_sem=send, recv_sem=recv,
            device_id={"tile": target}, device_id_type=MESH,
        )

    def piece(s, sh, b0, n, mine):
        return own.at[s, pl.ds(b0, n)] if mine else gath.at[s, sh, pl.ds(b0, n)]

    def send(table, s, sh, target, sem, mine, cond=None):
        def go(runs):
            for b0, n in runs:
                rc(piece(s, sh, b0, n, mine), gath.at[s, sh, pl.ds(b0, n)], target, sem, r_sem.at[s, sh]).start()
        by_chip(table, go, cond)

    def sent(table, s, sem, cond=None):
        def go(runs):
            n = count(runs)
            src = own.at[s, pl.ds(0, n)]
            rc(src, gath.at[s, me, pl.ds(0, n)], other, sem, r_sem.at[s, me]).wait_send()
        by_chip(table, go, cond)

    def arrived(table, s, sh, cond=None):
        def go(runs):
            n = count(runs)
            dst = gath.at[s, sh, pl.ds(0, n)]
            rc(dst, dst, other, lc.at[s], r_sem.at[s, sh]).wait_recv()
        by_chip(table, go, cond)

    def each(body, steps, start=0):
        def step(i, carry):
            body(i)
            return carry
        lax.fori_loop(start, steps, step, 0)

    def spread(s, n):
        if isinstance(n, int) and n in (0, slots):
            return n == slots
        return ((s + 1) * n) // slots > (s * n) // slots

    def turns_up(zi, yi, s):
        return spread(s, lookup(plan.turn_up, zi * Y + yi))

    def turns_down(zi, yi, s):
        return spread(s, lookup(plan.turn_down, zi * Y + yi))

    any_up = any(plan.turn_up)
    any_down = any(plan.turn_down)

    def vis_copy(s, u):
        return pltpu.make_async_copy(vis.at[u, s], work.at[s, u], vsem.at[s, u])

    def res_copy(s, u):
        return pltpu.make_async_copy(work.at[s, u], res.at[u, s], osem.at[s, u])

    def kept(u):
        return lookup([int(k) for k in plan.kept[u]], me) == 1

    all_kept = [all(k) for k in plan.kept]
    extra_id = lookup(plan.extra, me)
    extra_home = extra_id // units
    extra_row = extra_id % units

    def lend(s, u):
        target = lookup([plan.worker[t * units + u] for t in range(T)], me)
        return rc(vis.at[u, s], work.at[s, units], target, ms.at[s, u], mr.at[s])

    def give_back(s):
        return rc(work.at[s, units], res.at[extra_row, s], extra_home, ks.at[s], kr.at[s, extra_row])

    barrier = pltpu.get_barrier_semaphore()
    each(lambda k: pl.semaphore_signal(
        barrier, inc=1, device_id={"tile": (me + k + 1) % T}, device_id_type=MESH), T - 1)

    def up(s, zi, yi, mine=False, cond=None):
        cond = both(z < Z - 1, cond)
        send(plan.up, s, dev(zi, yi, core), dev(z + 1, y, core), su.at[s, zi * Y + yi], mine, cond)

    def down(s, zi, yi, mine=False, cond=None):
        cond = both(z > 0, cond)
        send(plan.down, s, dev(zi, yi, core), dev(z - 1, y, core), sd.at[s, zi * Y + yi], mine, cond)

    def mate(s, zi, yi, mine=False, cond=None):
        send(plan.need, s, dev(zi, yi, core), other, sc.at[s, zi * Y + yi], mine, cond)

    def pick_first(zi, yi, s, body):
        for u_ in ((False, True) if any_up else (False,)):
            for d_ in ((False, True) if any_down else (False,)):
                conds = []
                if any_up:
                    t = turns_up(zi, yi, s)
                    conds.append(t if u_ else negate(t))
                if any_down:
                    t = turns_down(zi, yi, s)
                    conds.append(t if d_ else negate(t))
                body(plan.first[u_, d_], both(*conds) if conds else None)

    def own_z(s):
        up(s, z, y, True)
        down(s, z, y, True)

    def own_side(s):
        if Y > 1:
            pick_first(z, y, s, lambda table, cond: send(
                table, s, me, dev(z, yother, core), sy.at[s, z], True, cond))
        mate(s, z, y, True)
        pltpu.make_async_copy(own.at[s], gath.at[s, me], lc.at[s]).start()

    pool_size = dirs.shape[1]
    slot_lane = lax.broadcasted_iota(jnp.int32, (per_group, 128), 1)
    pool_lane = lax.broadcasted_iota(jnp.int32, (per_group, pool_size), 1).astype(jnp.float32)

    same = lax.broadcasted_iota(jnp.int32, (per_group, per_group), 0) == lax.broadcasted_iota(
        jnp.int32, (per_group, per_group), 1)

    def make_factors(s):
        at_slot = slot_lane == s
        row = listed[pl.ds(s, 1), :].astype(jnp.float32)
        index = jnp.sum(jnp.where(same, row, 0.0), axis=1, keepdims=True)
        chosen = pool_lane == index

        def pick(row):
            return jnp.sum(jnp.where(chosen, row, 0.0), axis=1, keepdims=True)

        east = pick(dirs[0:1, :])
        north = pick(dirs[1:2, :])
        bacc[...] += jnp.where(at_slot, pick(pool_flux[...].astype(jnp.float32).reshape(1, pool_size)), 0.0)
        depth = jnp.sqrt(1.0 - east * east - north * north) - 1.0
        for b in range(BLOCKS):
            cut = slice(b * span, (b + 1) * span)
            turns = uvw[0, pl.ds(s, 1), cut] * east + uvw[1, pl.ds(s, 1), cut] * north + uvw[2, pl.ds(s, 1), cut] * depth
            sine, cosine = sin_cos_turns(turns)
            b0 = beam[s, 0, :, cut].astype(jnp.float32)
            b1 = beam[s, 1, :, cut].astype(jnp.float32)
            own[s, b, :per_group] = (b0 * cosine + b1 * sine).astype(jnp.bfloat16)
            own[s, b, per_group:] = (b1 * cosine - b0 * sine).astype(jnp.bfloat16)

    bacc[...] = jnp.zeros_like(bacc)
    make_factors(0)
    pl.semaphore_wait(barrier, T - 1)
    def lend_step(s):
        for u in range(units):
            if not all_kept[u]:
                pl.when(jnp.logical_not(kept(u)))(lambda: lend(s, u).start())

    def at_end():
        if isinstance(z, int):
            return z in (0, Z - 1)
        return jnp.logical_or(z == 0, z == Z - 1)

    starts = (
        (min(END_AHEAD, slots), at_end, own_z),
        (min(AHEAD, slots), lambda: negate(at_end()), own_z),
        (min(SIDE_AHEAD, slots), None, own_side),
        (min(LEND_AHEAD, slots), None, lend_step),
    )

    def make_and_send(s):
        make_factors(s + 1)

        for lead, cond, body in starts:
            early = s < lead
            when(both(early, cond and cond()))(functools.partial(body, s))
    each(make_and_send, slots - 1)
    square = jnp.concatenate([bacc[...], jnp.zeros((128 - per_group, 128), jnp.float32)], axis=0)
    bright[...] = square.T[:16].astype(jnp.bfloat16)
    flx[...] = jnp.zeros_like(flx)
    for lead, cond, body in starts:
        if lead == slots:
            when(cond and cond())(functools.partial(body, slots - 1))

    def bright_step(k):
        target = (me + k + 1) % T
        rc(bright, ball.at[me], target, bs.at[k], br.at[me]).start()
    each(bright_step, T - 1)
    ball[me] = bright[...]

    def vis_step(s):
        for u in range(units):
            if all_kept[u]:
                vis_copy(s, u).start()
            else:
                pl.when(kept(u))(lambda: vis_copy(s, u).start())
    each(vis_step, slots)

    def z_one(zi, s, upward):
        sh = dev(zi, y, core)
        arrived(plan.from_below if upward else plan.from_above, s, sh)
        (up if upward else down)(s, zi, y)
        if Y > 1:
            cond = None
            if upward and any_up:
                cond = negate(turns_up(zi, y, s))
            if not upward and any_down:
                cond = negate(turns_down(zi, y, s))
            send(plan.across, s, sh, dev(z, yother, core), sy.at[s, zi], False, cond)
        mate(s, zi, y)

    def z_step(d, s):
        when(z - d >= 0)(lambda: z_one(z - d, s, True))
        when(z + d < Z)(lambda: z_one(z + d, s, False))

    def y_far(zi, s, upward):
        sh = dev(zi, yother, core)
        if any_up if upward else any_down:
            turned = (turns_up if upward else turns_down)(zi, yother, s)

            @when(turned)
            def _():
                arrived(plan.from_below if upward else plan.from_above, s, sh)
                (up if upward else down)(s, zi, yother)
            arrived(plan.need, s, sh, negate(turned))
        else:
            arrived(plan.need, s, sh)
        mate(s, zi, yother)

    def y_near(s):
        sh = dev(z, yother, core)

        def go(table, cond):
            arrived([table[plan.pair[c]] for c in range(Z * Y)], s, sh, cond)
        pick_first(z, yother, s, go)
        if any_up:
            up(s, z, yother, cond=turns_up(z, yother, s))
        if any_down:
            down(s, z, yother, cond=turns_down(z, yother, s))
        mate(s, z, yother)

    def y_step(d, s):
        if Y == 1:
            return
        if d == 0:
            y_near(s)
            return
        when(z - d >= 0)(lambda: y_far(z - d, s, True))
        when(z + d < Z)(lambda: y_far(z + d, s, False))

    def bright_wait(k):
        src = (me + k + 1) % T
        rc(bright, ball.at[src], other, bs.at[k], br.at[src]).wait_recv()

    rows = T * 2 * per_group
    split = (T, 2, per_group, span)

    def turn(a):
        a4 = a.reshape(split)
        return jnp.concatenate([a4[:, 1:], -a4[:, :1]], axis=1).reshape(rows, span)

    def tn(a, b):
        return lax.dot_general(a, b, (((0,), (0,)), ((), ())), preferred_element_type=jnp.float32)

    def nt(a, b):
        return lax.dot_general(a, b, (((1,), (1,)), ((), ())), preferred_element_type=jnp.float32)

    def nn(a, b):
        return lax.dot_general(a, b, (((1,), (0,)), ((), ())), preferred_element_type=jnp.float32)

    def compute(s):
        lane = lax.broadcasted_iota(jnp.int32, (T, per_group, 128), 2)
        here = lane == s
        bcol = jnp.sum(jnp.where(here, bcols[...], 0.0), axis=2, keepdims=True)

        def block(b):
            return gath[s, :, b].reshape(rows, span)

        def scaled_of(f):
            f4 = f.reshape(split).astype(jnp.float32)
            return (f4 * bcol[:, None]).astype(jnp.bfloat16).reshape(rows, span)

        def keep_row(t, b):
            start = pl.multiple_of(b * span, span)
            return 1.0 - flags[pl.ds(t, 1), pl.ds(start, span)].astype(jnp.float32)

        def flag_rows(b):
            return jnp.broadcast_to(keep_row(s, b), (span, span)).T

        def add_flux(x, u, v):
            w = x.astype(jnp.float32) * u + turn(x).astype(jnp.float32) * v
            w = w.reshape(split)
            w = jnp.sum(w, axis=1)
            total = jnp.sum(w, axis=2, keepdims=True)
            flx[...] += jnp.where(here, total, 0.0)

        def unit(u, unit_id):
            p, q, diag = unit_blocks(unit_id)

            @pl.when(jnp.logical_not(diag))
            def _():
                x = block(p)
                c = block(q)
                sx = scaled_of(x)
                w = flag_rows(p) * keep_row(s, q)
                rre = (w * (work[s, u, 0].astype(jnp.float32) - tn(sx, c))).astype(jnp.bfloat16)
                rim = (w * (work[s, u, 1].astype(jnp.float32) - tn(turn(sx), c))).astype(jnp.bfloat16)
                work[s, u, 0] = rre
                work[s, u, 1] = rim
                add_flux(x, nt(c, rre), nt(c, rim))

            @pl.when(diag)
            def _():
                x = block(p)
                c = block(q)
                rid = lax.broadcasted_iota(jnp.int32, (span, span), 0)
                cid = lax.broadcasted_iota(jnp.int32, (span, span), 1)
                hi = rid < cid
                lo = rid > cid
                sx = scaled_of(x)
                sb = scaled_of(c)
                pre = jnp.where(hi, tn(sx, x), tn(c, sb))
                pim = jnp.where(hi, tn(turn(sx), x), tn(c, turn(sb)))
                w = jnp.where(hi, flag_rows(p) * keep_row(s, p), 0.0) + jnp.where(
                    lo, flag_rows(q) * keep_row(s, q), 0.0)
                rre = (w * (work[s, u, 0].astype(jnp.float32) - pre)).astype(jnp.bfloat16)
                rim = (w * (work[s, u, 1].astype(jnp.float32) - pim)).astype(jnp.bfloat16)
                work[s, u, 0] = rre
                work[s, u, 1] = rim
                zero = jnp.zeros((span, span), jnp.float32)

                def part(r, m):
                    return jnp.where(m, r.astype(jnp.float32), zero).astype(jnp.bfloat16)
                add_flux(x, nt(x, part(rre, hi)), nt(x, part(rim, hi)))
                add_flux(c, nn(c, part(rre, lo)), nn(c, part(rim, lo)))

        def run(u):
            lent = u == units
            active = jnp.logical_and(lent, extra_id >= 0)
            for k in range(units):
                mine = u == k
                active = jnp.logical_or(active, mine if all_kept[k] else jnp.logical_and(mine, kept(k)))

            @pl.when(active)
            def _():
                @pl.when(lent)
                def _():
                    rc(work.at[s, units], work.at[s, units], other, ks.at[s], mr.at[s]).wait_recv()

                @pl.when(jnp.logical_not(lent))
                def _():
                    vis_copy(s, jnp.where(lent, 0, u)).wait()
                unit(u, jnp.where(lent, extra_id, me * units + u))

                @pl.when(lent)
                def _():
                    give_back(s).start()

                @pl.when(jnp.logical_not(lent))
                def _():
                    res_copy(s, jnp.where(lent, 0, u)).start()

        if plan.moves:
            each(lambda k: run(units - k), units + 1)
        else:
            each(run, units)

    def last_step(s):
        @pl.when(s == 0)
        def _():
            each(bright_wait, T - 1)

            def unfold(k):
                rows_in = ball[k].astype(jnp.float32)
                square = jnp.concatenate([rows_in, jnp.zeros((112, 128), jnp.float32)], axis=0)
                bcols[k] = square.T[:per_group]
            each(unfold, T)
        pltpu.make_async_copy(own.at[s], gath.at[s, me], lc.at[s]).wait()

        compute(s)

    def mates(s):
        if isinstance(chip, int):
            for i in range(T // 2):
                arrived(plan.need, s, 2 * i + 1 - core)
            return
        each(lambda i: arrived(plan.need, s, 2 * i + 1 - core), T // 2)

    hop_lag = HOP_LAG
    final_lag = max(Z - 2, 0) * hop_lag + Y_LAG + FINAL_EXTRA

    def at(t, lag, body, cond=None):
        s = t - lag
        due = jnp.logical_and(s >= 0, s < slots)

        @when(both(due, cond))
        def _():
            body(s)

    def transfers(t):
        for lead, cond, body in starts:
            if lead < slots:
                at(t, -lead, body, cond and cond())
        for d in range(1, Z):
            at(t, (d - 1) * hop_lag, functools.partial(z_step, d))
        at(t, NEAR_LAG, lambda s: y_step(0, s))
        for d in range(1, Z):
            at(t, (d - 1) * hop_lag + Y_LAG, functools.partial(y_step, d))
        at(t, final_lag, mates)

    def tick(t):
        if Z * Y <= 8:
            for k in range(Z * Y):
                pl.when(chip == k)(lambda: placed(k, lambda: transfers(t)))
        else:
            transfers(t)
        at(t, final_lag, last_step)

    each(tick, slots + final_lag)

    sharing = 128 // per_group
    turned_flux = flx[...].reshape(T * per_group, 128).T[:slots]
    for k in range(T // sharing):
        fsend[k] = turned_flux[:, k * 128:(k + 1) * 128]

    def flux_step(k):
        target = (me + k + 1) % T
        rc(fsend.at[target // sharing], frecv.at[me], target, fs.at[k], fr.at[me]).start()
    each(flux_step, T - 1)
    frecv[me] = fsend[me // sharing]

    def tidy(s):
        for u in range(units):
            if all_kept[u]:
                res_copy(s, u).wait()
            else:
                pl.when(kept(u))(lambda: res_copy(s, u).wait())

                @pl.when(jnp.logical_not(kept(u)))
                def _():
                    lend(s, u).wait_send()
                    rc(work.at[s, units], res.at[u, s], other, ks.at[s], kr.at[s, u]).wait_recv()
        if plan.moves:
            @pl.when(extra_id >= 0)
            def _():
                rc(work.at[s, units], res.at[0, s], other, ks.at[s], kr.at[s, 0]).wait_send()

        def from_row(zi):
            def z_sent(yi, extra_up, extra_down):
                sent(plan.up, s, su.at[s, zi * Y + yi], both(zi <= z, z < Z - 1, *extra_up))
                sent(plan.down, s, sd.at[s, zi * Y + yi], both(zi >= z, z > 0, *extra_down))

            z_sent(y, (), ())
            if Y > 1:
                if any_up:
                    sent(plan.up, s, su.at[s, zi * Y + yother], both(zi <= z, z < Z - 1, turns_up(zi, yother, s)))
                if any_down:
                    sent(plan.down, s, sd.at[s, zi * Y + yother], both(zi >= z, z > 0, turns_down(zi, yother, s)))

                @pl.when(zi == z)
                def _():
                    pick_first(z, y, s, lambda table, cond: sent(table, s, sy.at[s, zi], cond))
                below = zi < z
                if any_up:
                    below = both(below, jnp.logical_not(turns_up(zi, y, s)))
                sent(plan.across, s, sy.at[s, zi], below)
                above = zi > z
                if any_down:
                    above = both(above, jnp.logical_not(turns_down(zi, y, s)))
                sent(plan.across, s, sy.at[s, zi], above)
            for yi in range(Y):
                sent(plan.need, s, sc.at[s, zi * Y + yi])
        each(from_row, Z)
    each(tidy, slots)

    def small_wait(k):
        src = (me + k + 1) % T
        rc(bright, ball.at[me], src, bs.at[k], br.at[me]).wait_send()
        one = rc(fsend.at[src // sharing], frecv.at[src], src, fs.at[k], fr.at[src])
        one.wait_send()
        one.wait_recv()
    each(small_wait, T - 1)
    total = jnp.sum(frecv[...], axis=0) * scale
    mine = total[:, :per_group]
    for k in range(1, sharing):
        mine = jnp.where(me % sharing == k, total[:, k * per_group:(k + 1) * per_group], mine)
    flux[...] = mine


def per_device(
    layout, visibility, station_beam, antenna_uvw, source_dirs, source_flux, visible_list, antenna_flags
):
    Z, Y = layout
    T = lax.axis_size("tile")
    units, slots, _, span, _ = visibility.shape
    per_group = station_beam.shape[2]
    antennas = station_beam.shape[3]
    dims = (Z, Y, slots, units, per_group, span, -1.0 / (8.0 * antennas))
    plan = Plan(Z, Y, units)
    vmem = pl.BlockSpec(memory_space=pltpu.VMEM)
    hbm = pl.BlockSpec(memory_space=pl.ANY)
    dma = pltpu.SemaphoreType.DMA
    residual, flux = pl.pallas_call(
        functools.partial(kernel, dims, plan),
        name="predict_pull",
        out_shape=(
            pltpu.VMEM(visibility.shape, jnp.bfloat16),
            pltpu.VMEM((slots, per_group), jnp.float32),
        ),
        in_specs=[vmem] * 6 + [hbm],
        out_specs=(vmem, vmem),
        scratch_shapes=[
            pltpu.VMEM((slots, BLOCKS, 2 * per_group, span), jnp.bfloat16),
            pltpu.VMEM((per_group, 128), jnp.float32),
            pltpu.VMEM((16, 128), jnp.bfloat16),
            pltpu.VMEM((slots, T, BLOCKS, 2 * per_group, span), jnp.bfloat16),
            pltpu.VMEM((T, 16, 128), jnp.bfloat16),
            pltpu.VMEM((slots, units + 1, 2, span, span), jnp.bfloat16),
            pltpu.VMEM((T, per_group, 128), jnp.float32),
            pltpu.VMEM((T * per_group // 128, slots, 128), jnp.float32),
            pltpu.VMEM((T, slots, 128), jnp.float32),
            pltpu.VMEM((T, per_group, 128), jnp.float32),
            dma((slots, T)),
            dma((slots, Z * Y)),
            dma((slots, Z * Y)),
            dma((slots, Z)),
            dma((slots, Z * Y)),
            dma((slots,)),
            dma((slots, units)),
            dma((slots, units)),
            dma((T,)),
            dma((T,)),
            dma((T,)),
            dma((T,)),
            dma((slots, units)),
            dma((slots,)),
            dma((slots,)),
            dma((slots, units)),
        ],
        compiler_params=pltpu.CompilerParams(
            collective_id=0, has_side_effects=True, vmem_limit_bytes=54 * 1024 * 1024
        ),
    )(station_beam, antenna_uvw.transpose(1, 0, 2), source_dirs, source_flux, visible_list, antenna_flags, visibility)
    return residual, flux


def layout_of(mesh):
    count = mesh.shape["tile"]
    line = mesh.devices.reshape(-1, count)[0]
    places = [getattr(d, "coords", None) for d in line]
    fast = 1
    if all(c is not None for c in places):
        fast = max(1, len({tuple(c)[1] for c in places}))
    if (count // 2) % fast or fast > 2:
        fast = 1
    return count // 2 // fast, fast


def solution(mesh):
    return jax.shard_map(
        functools.partial(per_device, layout_of(mesh)),
        mesh=mesh,
        in_specs=(
            P("tile", "grp", None, None, None),
            P("grp", None, "tile", None),
            P("grp", None, None),
            P(None, "tile"),
            P(("grp", "tile")),
            P(None, "tile"),
            P("grp", None),
        ),
        out_specs=(P("tile", "grp", None, None, None), P("grp", "tile")),
        check_vma=False,
    )
```
